512 devices in a mesh: lat: 64 (over y, z), wid: 8 (over x, core).
Axes of the slice: x: 4, y: 4, z: 16, core: 2. Of those that a mesh axis runs over, the one named last changes fastest.
Arguments:
- activations: bfloat16 [128, 3584], P(None, 'wid'), may hold values from -6 to 6
- encoder: bfloat16 [3584, 32768], P('wid', 'lat'), may hold values from -0.09375 to 0.09375
- encoder_bias: float32 [32768], P('lat'), may hold values from -3 to 3
- decoder: bfloat16 [32768, 3584], P('lat', 'wid'), may hold values from -0.75 to 0.75
- decoder_bias: float32 [3584], P('wid'), may hold values from -3 to 3
- kept_mask: int32 [128, 32768], P(None, 'lat'), may hold values 0 or 1
- boundaries: int32 [8], replicated, may hold values from 4097 to 32768, as said below
Outputs:
- encoder_grad: bfloat16 [3584, 32768], P('wid', 'lat')
- encoder_bias_grad: float32 [32768], P('lat')
- decoder_grad: bfloat16 [32768, 3584], P('lat', 'wid')
- decoder_bias_grad: float32 [3584], P('wid')
The draws below stay inside these ranges and needn't reach their ends.
Inputs may be any that keep to these rules, and one draw needn't show every extreme that they name: `boundaries`: Rising; for k below 7, boundary k lies among the 512 latents that follow (k + 1) * 4096; the last equals 32768.
All inputs are finite; a program needn't handle non-finite values. No bound on the sum of `kept_mask` on one device may be relied on, other than what follows from the above.
Results may differ from the reference program's by a relative error of at most 0.006.
Values may be sent and summed in bfloat16 or wider, within the bound.
No kernel may reach another device: no remote copies, remote signals or barrier semaphores. Data moves between devices by JAX's collectives and lax.ppermute only.
A program may use at most 128 MiB of HBM per device.

```python
import jax
import jax.numpy as jnp
from jax import lax

D = 3584
LAT_DEV = 512
TOKENS = 128
GROUPS = 8
KEEP = 64
LATENTS = 32768
N_LAT = 64


def draw_boundaries(key, part):
    span_width = LATENTS // GROUPS
    jitter = jax.random.randint(key, (GROUPS,), 0, LAT_DEV)
    range_starts = jnp.arange(1, GROUPS + 1, dtype=jnp.int32) * span_width
    final_slot = jnp.arange(GROUPS) == GROUPS - 1
    return jnp.where(final_slot, LATENTS, range_starts + 1 + jitter).astype(jnp.int32)


def plant(array, rng, low, top_value):
    shape = array.shape
    index_at = [jax.random.randint(jax.random.fold_in(rng, axis), (), 0, shape[axis]) for axis in range(len(shape))]
    array = array.at[tuple(index_at)].set(low)
    longest = shape.index(max(shape))
    index_at[longest] = (index_at[longest] + 1) % shape[longest]
    return array.at[tuple(index_at)].set(top_value)


def shard_levels(key, extent, cuts, smallest, top_value):
    def one(axis_at, blocks):
        draws = jax.random.uniform(jax.random.fold_in(jax.random.fold_in(key, 6), axis_at), (blocks,), jnp.float32, smallest / len(cuts), top_value / len(cuts))
        return jnp.repeat(jnp.exp(draws), extent[axis_at] // blocks).reshape((-1,) + (1,) * (len(extent) - axis_at - 1))

    loudness = one(*cuts[0])
    for cut in cuts[1:]:
        loudness = loudness * one(*cut)
    return loudness


def noise(own_key, dims, scale, limit, shards=(), kind=jnp.bfloat16):
    array = scale * jax.random.normal(own_key, dims, jnp.float32)
    if shards:
        array = array * shard_levels(own_key, dims, shards, -0.22, 0.18)
    return jnp.clip(array, -limit, limit).astype(kind)


def setup_inputs(seed: int = 0) -> dict:
    keys = jax.random.split(jax.random.key(seed), 8)
    activations = noise(keys[0], (TOKENS, D), 1.0, 6.0, ((1, 8),))
    encoder = noise(keys[1], (D, LATENTS), D ** -0.5, 0.09375, ((0, 8), (1, 64)))
    encoder_bias = noise(keys[2], (LATENTS,), 0.5, 3.0, ((0, 64),), jnp.float32)
    decoder = noise(keys[3], (LATENTS, D), KEEP ** -0.5, 0.75, ((0, 64), (1, 8)))
    decoder_bias = noise(keys[4], (D,), 0.5, 3.0, ((0, 8),), jnp.float32)
    kept_mask = plant((jax.random.randint(keys[5], (TOKENS, LATENTS), 0, LATENTS) < KEEP).astype(jnp.int32), jax.random.fold_in(keys[5], 1), 0, 1)
    boundaries = draw_boundaries(jax.random.fold_in(keys[7], 71), 0)
    return {"activations": activations, "encoder": encoder, "encoder_bias": encoder_bias, "decoder": decoder, "decoder_bias": decoder_bias, "kept_mask": kept_mask, "boundaries": boundaries}


def block_product(operands):
    return jnp.dot(operands[0], operands[1], preferred_element_type=jnp.float32)


def block_back(operands):
    return jnp.dot(operands[0], operands[1].T, preferred_element_type=jnp.float32)


def block_outer(operands):
    return jnp.dot(operands[0].T, operands[1], preferred_element_type=jnp.float32)


def reference(activations, encoder, encoder_bias, decoder, decoder_bias, kept_mask, boundaries):
    preacts = jnp.dot(activations, encoder, preferred_element_type=jnp.float32) + encoder_bias
    kept_float = kept_mask.astype(jnp.float32)
    codes = (kept_float * preacts).astype(jnp.bfloat16)
    code_blocks = jnp.transpose(codes.reshape(TOKENS, N_LAT, LAT_DEV), (1, 0, 2))
    decoder_blocks = decoder.reshape(N_LAT, LAT_DEV, D)
    totals = lax.map(block_product, (code_blocks, decoder_blocks))
    earlier = jnp.concatenate([jnp.zeros((1, TOKENS, D), jnp.float32), jnp.cumsum(totals, axis=0)[:-1]], axis=0)
    local_ids = jnp.arange(LAT_DEV, dtype=jnp.int32)
    target_rows = activations.astype(jnp.float32)
    error_list = []
    for boundary in range(GROUPS):
        cut_point = boundaries[boundary].astype(jnp.int32)
        block_index = ((cut_point - 1) // LAT_DEV).astype(jnp.int32)
        block_codes = lax.dynamic_index_in_dim(code_blocks, block_index, 0, keepdims=False)
        block_decoder = lax.dynamic_index_in_dim(decoder_blocks, block_index, 0, keepdims=False)
        below_cut = (block_index * LAT_DEV + local_ids) < cut_point
        masked_codes = jnp.where(below_cut[None, :], block_codes, jnp.zeros((), jnp.bfloat16))
        recon = decoder_bias + earlier[block_index] + block_product((masked_codes, block_decoder))
        error_list.append(recon - target_rows)
    errors = jnp.stack(error_list)
    suffix = jnp.cumsum(errors[::-1], axis=0)[::-1] / GROUPS
    suffix_low = suffix.astype(jnp.bfloat16)
    padded = jnp.concatenate([suffix_low, jnp.zeros((1, TOKENS, D), jnp.bfloat16)], axis=0)
    block_starts = jnp.arange(N_LAT, dtype=jnp.int32) * LAT_DEV
    start_group = jnp.sum((boundaries[None, :] <= block_starts[:, None]).astype(jnp.int32), axis=1)
    block_suffix = padded[start_group]
    code_grads = lax.map(block_back, (block_suffix, decoder_blocks))
    decoder_grads = lax.map(block_outer, (code_blocks, block_suffix))
    for boundary in range(GROUPS):
        cut_point = boundaries[boundary].astype(jnp.int32)
        block_index = ((cut_point - 1) // LAT_DEV).astype(jnp.int32)
        block_codes = lax.dynamic_index_in_dim(code_blocks, block_index, 0, keepdims=False)
        block_decoder = lax.dynamic_index_in_dim(decoder_blocks, block_index, 0, keepdims=False)
        above_cut = (block_index * LAT_DEV + local_ids) >= cut_point
        later_suffix = padded[boundary + 1]
        fixed_codes = jnp.where(above_cut[None, :], block_back((later_suffix, block_decoder)), code_grads[block_index])
        code_grads = code_grads.at[block_index].set(fixed_codes)
        fixed_rows = jnp.where(above_cut[:, None], block_outer((block_codes, later_suffix)), decoder_grads[block_index])
        decoder_grads = decoder_grads.at[block_index].set(fixed_rows)
    code_grad_all = jnp.transpose(code_grads, (1, 0, 2)).reshape(TOKENS, LATENTS)
    pre_grads = kept_float * code_grad_all
    encoder_bias_grad = jnp.sum(pre_grads, axis=0)
    encoder_grad = jnp.dot(activations.T, pre_grads.astype(jnp.bfloat16), preferred_element_type=jnp.float32).astype(jnp.bfloat16)
    decoder_grad = decoder_grads.reshape(LATENTS, D).astype(jnp.bfloat16)
    decoder_bias_grad = jnp.sum(suffix[0], axis=0)
    return (encoder_grad, encoder_bias_grad, decoder_grad, decoder_bias_grad)
```

```python
import jax
import jax.numpy as jnp
from jax import lax
from jax.sharding import PartitionSpec as P

GROUPS = 8
BF = jnp.bfloat16
F32 = jnp.float32
LANES = 128


def swap(x, axis):
    return lax.all_to_all(x, axis, 0, 0, tiled=False)


def spread(x, axis):
    count = lax.axis_size(axis)
    return swap(jnp.broadcast_to(x[None], (count,) + x.shape), axis)


def split_high_low(x):
    high = x.astype(BF)
    low = (x - high.astype(F32)).astype(BF)
    return high, low


def body(activations, encoder, encoder_bias, decoder, decoder_bias, kept_mask, boundaries):
    tokens, width = activations.shape
    latents = encoder.shape[1]
    n_lat, n_wid = lax.axis_size("lat"), lax.axis_size("wid")
    place = lax.axis_index("lat")
    part = lax.axis_index("wid")
    rows = tokens // n_wid
    own = tokens // n_lat
    span = n_lat // GROUPS
    group = place // span
    spare = -width % LANES
    share = width // n_lat

    has_cut = (place % span == 0) & (group > 0)
    cut_point = jnp.where(has_cut, boundaries[jnp.maximum(group - 1, 0)], 0)
    latent_ids = place * latents + jnp.arange(latents, dtype=jnp.int32)
    below_cut = (latent_ids < cut_point)[None, :]
    kept_rows = lax.dynamic_slice_in_dim(kept_mask, part * rows, rows, 0).astype(F32)

    enc_part = jnp.dot(activations, encoder, preferred_element_type=F32).astype(BF)
    pieces = swap(enc_part.reshape(n_wid, rows, latents), "wid")
    preacts = jnp.sum(pieces.astype(F32), axis=0) + encoder_bias
    my_codes = (kept_rows * preacts).astype(BF)
    codes = spread(my_codes, "wid").reshape(tokens, latents)

    zero = jnp.zeros((), BF)
    both_codes = jnp.stack([jnp.where(below_cut, codes, zero), jnp.where(below_cut, zero, codes)])
    decoded = jnp.einsum("sbj,jd->sbd", both_codes, decoder, preferred_element_type=F32)
    weight = (GROUPS - group).astype(F32) / GROUPS
    token_sums = jnp.sum(decoded, axis=1)
    bias_part = token_sums[0] * (weight + 1 / GROUPS) + token_sums[1] * weight
    tags = jnp.stack(split_high_low(bias_part.reshape(n_lat, share)), axis=1)
    sent = jnp.transpose(decoded.astype(BF).reshape(2, n_lat, own, width), (1, 0, 2, 3)).reshape(n_lat, 2 * own, width)
    tags = jnp.pad(tags, ((0, 0), (0, 2 * own - 2), (0, spare - share)))
    got = swap(jnp.concatenate([sent, tags], axis=2), "lat")
    bias_share = jnp.sum(got[:, :2, width : width + share].astype(F32), axis=(0, 1))

    pieces = got[:, :, :width].astype(F32).reshape(GROUPS, span, 2, own, width)
    high_sum = jnp.sum(pieces[:, :, 1], axis=1)
    low_sum = pieces[:, 0, 0]
    segment = high_sum + jnp.concatenate([low_sum[1:], jnp.zeros_like(low_sum[:1])], axis=0)
    target = lax.dynamic_slice_in_dim(activations, place * own, own, 0).astype(F32)
    run = decoder_bias - target
    errors = []
    for k in range(GROUPS):
        run = run + segment[k]
        errors.append(run)
    tail = jnp.zeros_like(run)
    suffixes = []
    for error in reversed(errors):
        tail = tail + error
        suffixes.append(tail / GROUPS)
    suffix = jnp.stack(suffixes[::-1]).astype(BF)
    before = jnp.concatenate([suffix[:1], suffix[:-1]], axis=0)
    pair = jnp.concatenate([before, suffix], axis=1)
    tags = jnp.stack(split_high_low(bias_share), axis=0)
    tags = jnp.pad(tags, ((0, 2 * own - 2), (0, spare - share)))
    pair = jnp.concatenate([pair, jnp.broadcast_to(tags[None], (GROUPS,) + tags.shape)], axis=2)
    back = jnp.broadcast_to(pair[:, None], (GROUPS, span) + pair.shape[1:]).reshape(n_lat, 2 * own, width + spare)
    mine = swap(back, "lat")
    bias_sum = jnp.sum(mine[:, :2, width : width + share].astype(F32), axis=1).reshape(width)
    decoder_bias_grad = bias_sum + tokens * decoder_bias - jnp.sum(activations.astype(F32), axis=0)

    suffix_pair = jnp.transpose(mine[:, :, :width].reshape(n_lat, 2, own, width), (1, 0, 2, 3)).reshape(2, tokens, width)
    back_grads = jnp.einsum("sbd,jd->sbj", suffix_pair, decoder, preferred_element_type=F32)
    partial_grads = jnp.where(below_cut, back_grads[0], back_grads[1]).astype(BF)
    pieces = swap(partial_grads.reshape(n_wid, rows, latents), "wid")
    my_grads = (kept_rows * jnp.sum(pieces.astype(F32), axis=0)).astype(BF)
    pre_low = spread(my_grads, "wid").reshape(tokens, latents)
    encoder_bias_grad = jnp.sum(pre_low.astype(F32), axis=0)
    encoder_grad = lax.dot_general(
        activations, pre_low, (((0,), (0,)), ((), ())), preferred_element_type=F32
    ).astype(BF)
    decoder_grad = jnp.einsum(
        "sbj,sbd->jd", both_codes, suffix_pair, preferred_element_type=F32
    ).astype(BF)
    return (encoder_grad, encoder_bias_grad, decoder_grad, decoder_bias_grad)


def solution(mesh):
    placed = (
        P(None, "wid"),
        P("wid", "lat"),
        P("lat"),
        P("lat", "wid"),
        P("wid"),
        P(None, "lat"),
        P(),
    )
    return jax.shard_map(
        body,
        mesh=mesh,
        in_specs=placed,
        out_specs=(P("wid", "lat"), P("lat"), P("lat", "wid"), P("wid")),
        check_vma=False,
    )
```

```python
import jax
import jax.numpy as jnp
from jax import lax
from jax.sharding import PartitionSpec as P

GROUPS = 8
BF = jnp.bfloat16
F32 = jnp.float32

N_Y, N_FAR, NEAR = 4, 4, 4
N_Z = N_FAR * NEAR
SLICES = N_Y * NEAR
NEAR_GROUPS = [[N_Z * y + NEAR * q + r for y in range(N_Y) for r in range(NEAR)] for q in range(N_FAR)]
FAR_GROUPS = [[N_Z * y + NEAR * q + r for q in range(N_FAR)] for y in range(N_Y) for r in range(NEAR)]
PIECE = 32


def swap(x, axis, groups=None):
    return lax.all_to_all(x, axis, 0, 0, axis_index_groups=groups, tiled=False)


def copies(x, count):
    return jnp.broadcast_to(x[None], (count,) + x.shape)


def dot(a, b, over):
    return lax.dot_general(a, b, (((over[0],), (over[1],)), ((), ())), preferred_element_type=F32)


def pad_rows(x, rows):
    return jnp.pad(x.reshape(SLICES, rows, x.shape[1]), ((0, 0), (0, PIECE - rows), (0, 0)))


def sum_codes(pieces, kept, bias):
    return (kept * (jnp.sum(pieces.astype(F32), axis=0) + bias)).astype(BF)


def sum_grads(pieces, kept):
    return (kept * jnp.sum(pieces.astype(F32), axis=0)).astype(BF)


def split_codes(codes, below):
    zero = jnp.zeros_like(codes)
    return jnp.where(below, codes, zero), jnp.where(below, zero, codes)


def decode(codes, below, dec_pad):
    low, high = split_codes(codes, below)
    shape = (SLICES, PIECE, codes.shape[0])
    decoded = [dot(dec_pad, part, (1, 1)).reshape(shape) for part in (low, high)]
    return jnp.concatenate(decoded, axis=1).astype(BF)


def near_sums(got):
    tokens = got.shape[-1]
    got = got.astype(F32).reshape(N_Y, NEAR, 2 * PIECE, tokens)
    high = jnp.sum(got[:, :, PIECE:], axis=1)
    return jnp.concatenate([got[:, 0, :PIECE], high], axis=1).astype(BF)


def suffixes_of(got, base, late, rows):
    got = got.astype(F32)
    low, high = got[:, :, :PIECE], got[:, :, PIECE:]
    run = base
    errors = []
    for y in range(N_Y):
        run = run + ((high[0, y] + high[1, y]) + low[2, y])
        errors.append(run)
        part = high[2, y] + high[3, y]
        run = run + (part + low[0, y + 1] if y + 1 < N_Y else part)
        errors.append(run)
    tail = jnp.zeros_like(base)
    suffix = []
    for error in reversed(errors):
        tail = tail + error
        suffix.append(tail / GROUPS)
    suffix = suffix[::-1]
    row = lax.broadcasted_iota(jnp.int32, base.shape, 0)
    lane = lax.broadcasted_iota(jnp.int32, base.shape, 1)
    token_sum = jnp.sum(suffix[0], axis=1, keepdims=True)
    token_row = jnp.sum(jnp.where(row == lane, token_sum, 0.0), axis=0, keepdims=True)
    token_high = token_row.astype(BF).astype(F32)
    out = []
    for y in range(N_Y):
        own = jnp.where(late, suffix[2 * y + 1], suffix[2 * y])
        previous = jnp.where(late, suffix[2 * y], suffix[max(2 * y - 1, 0)])
        previous = jnp.where(row == rows, token_high, jnp.where(row == rows + 1, token_row - token_high, previous))
        out += [jnp.concatenate([previous, own], axis=0).astype(BF)] * NEAR
    return jnp.stack(out)


def back(got, below, dec_pad):
    shape = (SLICES * PIECE, got.shape[-1])
    low, high = got[:, :PIECE].reshape(shape), got[:, PIECE:].reshape(shape)
    return jnp.where(below, dot(low, dec_pad, (0, 0)), dot(high, dec_pad, (0, 0))).astype(BF)


def body(activations, encoder, encoder_bias, decoder, decoder_bias, kept_mask, boundaries):
    tokens, width = activations.shape
    latents = encoder.shape[1]
    n_wid = lax.axis_size("wid")
    place = lax.axis_index("lat")
    part = lax.axis_index("wid")
    rows = tokens // n_wid
    piece = width // SLICES
    span = lax.axis_size("lat") // GROUPS
    group = place // span
    y, z = place // N_Z, place % N_Z
    my_slice = NEAR * y + z % NEAR
    late = z // NEAR >= N_FAR // 2

    has_cut = (place % span == 0) & (group > 0)
    cut_point = jnp.where(has_cut, boundaries[jnp.maximum(group - 1, 0)], 0)
    latent_ids = place * latents + jnp.arange(latents, dtype=jnp.int32)
    below = (latent_ids < cut_point)[None, :]
    kept_rows = lax.dynamic_slice_in_dim(kept_mask, part * rows, rows, 0).astype(F32)

    enc_part = dot(activations, encoder, (1, 0)).astype(BF)
    pieces = swap(enc_part.reshape(n_wid, rows, latents), "wid")
    dec_pad = pad_rows(decoder.T, piece).reshape(SLICES * PIECE, latents)
    target = lax.dynamic_index_in_dim(pad_rows(activations.T, piece), my_slice, 0, False).astype(F32)
    base = lax.dynamic_index_in_dim(pad_rows(decoder_bias[:, None], piece), my_slice, 0, False) - target
    my_codes = sum_codes(pieces, kept_rows, encoder_bias[None])
    codes = swap(copies(my_codes, n_wid), "wid").reshape(tokens, latents)

    got = swap(decode(codes, below, dec_pad), "lat", NEAR_GROUPS)
    got = swap(copies(near_sums(got), N_FAR), "lat", FAR_GROUPS)
    got = swap(suffixes_of(got, base, late, piece), "lat", NEAR_GROUPS)

    partial_grads = back(got, below, dec_pad)
    pieces = swap(partial_grads.reshape(n_wid, rows, latents), "wid")
    suffix_low = got[:, :piece].reshape(width, tokens)
    suffix_high = got[:, PIECE : PIECE + piece].reshape(width, tokens)
    low, high = split_codes(codes, below)
    decoder_grad = (dot(suffix_low, low, (1, 0)) + dot(suffix_high, high, (1, 0))).astype(BF).T
    tags = got[:, piece : piece + 2, :piece].astype(F32)
    decoder_bias_grad = (tags[:, 0] + tags[:, 1]).reshape(width)
    my_grads = sum_grads(pieces, kept_rows)
    pre_low = swap(copies(my_grads, n_wid), "wid").reshape(tokens, latents)
    encoder_bias_grad = jnp.sum(pre_low.astype(F32), axis=0)
    encoder_grad = dot(activations, pre_low, (0, 0)).astype(BF)
    return (encoder_grad, encoder_bias_grad, decoder_grad, decoder_bias_grad)


def solution(mesh):
    placed = (
        P(None, "wid"),
        P("wid", "lat"),
        P("lat"),
        P("lat", "wid"),
        P("wid"),
        P(None, "lat"),
        P(),
    )
    return jax.shard_map(
        body,
        mesh=mesh,
        in_specs=placed,
        out_specs=(P("wid", "lat"), P("lat"), P("lat", "wid"), P("wid")),
        check_vma=False,
    )
```

```python
import jax
import jax.numpy as jnp
from jax import lax
from jax.experimental import pallas as pl
from jax.experimental.pallas import tpu as pltpu
from jax.sharding import PartitionSpec as P

GROUPS = 8
BF = jnp.bfloat16
F32 = jnp.float32

N_Y, N_FAR, NEAR = 4, 4, 4
N_Z = N_FAR * NEAR
SLICES = N_Y * NEAR
NEAR_GROUPS = [[N_Z * y + NEAR * q + r for y in range(N_Y) for r in range(NEAR)] for q in range(N_FAR)]
FAR_GROUPS = [[N_Z * y + NEAR * q + r for q in range(N_FAR)] for y in range(N_Y) for r in range(NEAR)]
PIECE = 32
N_CORE, N_X = 2, 4
CORE_PAIRS = [(i, i ^ 1) for i in range(N_CORE * N_X)]
CHIP_GROUPS = [[N_CORE * x + c for x in range(N_X)] for c in range(N_CORE)]


def swap(x, axis, groups=None):
    return lax.all_to_all(x, axis, 0, 0, axis_index_groups=groups, tiled=False)


def copies(x, count):
    return jnp.broadcast_to(x[None], (count,) + x.shape)


def dot(a, b, over):
    return lax.dot_general(a, b, (((over[0],), (over[1],)), ((), ())), preferred_element_type=F32)


def pad_rows(x, rows):
    return jnp.pad(x.reshape(SLICES, rows, x.shape[1]), ((0, 0), (0, PIECE - rows), (0, 0)))


def call(stage, shapes, scalars, *arrays):
    n_in = len(arrays)

    def kernel(scalar_ref, *refs):
        values = [scalar_ref[i] for i in range(len(scalars))]
        outs = stage(*values, *[ref[...] for ref in refs[:n_in]])
        for ref, out in zip(refs[n_in:], outs, strict=True):
            if isinstance(out, list):
                for i, one in enumerate(out):
                    ref[i] = one
            else:
                ref[...] = out

    vmem = pl.BlockSpec(memory_space=pltpu.VMEM)
    return pl.pallas_call(
        kernel,
        out_shape=[jax.ShapeDtypeStruct(shape, dtype) for shape, dtype in shapes],
        in_specs=[pl.BlockSpec(memory_space=pltpu.SMEM)] + [vmem] * n_in,
        out_specs=[vmem] * len(shapes),
        compiler_params=pltpu.CompilerParams(vmem_limit_bytes=32 * 1024 * 1024),
        name=stage.__name__,
    )(jnp.stack([jnp.asarray(v, jnp.int32) for v in scalars]), *arrays)


def half_of(core, x, other=False):
    half = x.shape[0] // N_CORE
    first = core == (1 if other else 0)
    return jnp.where(first, x[:half], x[half:])


def joined(core, own, other):
    own, other = own.astype(F32), other.astype(F32)
    return jnp.concatenate([jnp.where(core == 0, own, other), jnp.where(core == 0, other, own)], axis=0)


def split_codes(codes, cut):
    below = lax.broadcasted_iota(jnp.int32, codes.shape, 1) < cut
    return jnp.where(below, codes, 0.0).astype(BF), jnp.where(below, 0.0, codes).astype(BF)


def encode(core, activations, encoder):
    part = dot(activations, encoder, (0, 0))
    return half_of(core, part), half_of(core, part, True)


def pair_sum(core, kept, got):
    return ([(kept + got).astype(BF)] * N_X,)


def kept_codes(core, pieces, mask, bias):
    total = jnp.sum(pieces.astype(F32), axis=0) + bias
    return ((half_of(core, mask).astype(F32) * total).astype(BF),)


def kept_grads(core, pieces, mask):
    return ((half_of(core, mask).astype(F32) * jnp.sum(pieces.astype(F32), axis=0)).astype(BF),)


def decode(core, cut, own, other, dec_pad):
    codes = joined(core, own, other)
    shape = (SLICES, PIECE, codes.shape[0])
    decoded = [dot(dec_pad, part, (1, 1)).reshape(shape) for part in split_codes(codes, cut)]
    return (jnp.concatenate(decoded, axis=1).astype(BF),)


def near_sums(core, got):
    tokens = got.shape[-1]
    got = got.astype(F32).reshape(N_Y, NEAR, 2 * PIECE, tokens)
    high = jnp.sum(got[:, :, PIECE:], axis=1)
    return ([jnp.concatenate([got[:, 0, :PIECE], high], axis=1).astype(BF)] * N_FAR,)


def suffixes(late, rows, got, base):
    got = got.astype(F32)
    low, high = got[:, :, :PIECE], got[:, :, PIECE:]
    run = base
    errors = []
    for y in range(N_Y):
        run = run + ((high[0, y] + high[1, y]) + low[2, y])
        errors.append(run)
        part = high[2, y] + high[3, y]
        run = run + (part + low[0, y + 1] if y + 1 < N_Y else part)
        errors.append(run)
    tail = jnp.zeros_like(base)
    suffix = []
    for error in reversed(errors):
        tail = tail + error
        suffix.append(tail / GROUPS)
    suffix = suffix[::-1]
    row = lax.broadcasted_iota(jnp.int32, base.shape, 0)
    lane = lax.broadcasted_iota(jnp.int32, base.shape, 1)
    token_sum = jnp.sum(suffix[0], axis=1, keepdims=True)
    token_row = jnp.sum(jnp.where(row == lane, token_sum, 0.0), axis=0, keepdims=True)
    token_high = token_row.astype(BF).astype(F32)
    out = []
    for y in range(N_Y):
        own = jnp.where(late == 1, suffix[2 * y + 1], suffix[2 * y])
        previous = jnp.where(late == 1, suffix[2 * y], suffix[max(2 * y - 1, 0)])
        previous = jnp.where(row == rows, token_high, jnp.where(row == rows + 1, token_row - token_high, previous))
        out += [jnp.concatenate([previous, own], axis=0).astype(BF)] * NEAR
    return (out,)


def back(core, cut, got, dec_pad):
    tokens = got.shape[-1]
    got = got.astype(F32)
    low = got[:, :PIECE].reshape(SLICES * PIECE, tokens).astype(BF)
    high = got[:, PIECE:].reshape(SLICES * PIECE, tokens).astype(BF)
    low, high = dot(low, dec_pad, (0, 0)), dot(high, dec_pad, (0, 0))
    below = lax.broadcasted_iota(jnp.int32, low.shape, 1) < cut
    part = jnp.where(below, low, high)
    return half_of(core, part), half_of(core, part, True)


def encoder_grads(core, own, other, activations):
    grads = joined(core, own, other)
    return dot(activations, grads.astype(BF), (1, 0)).astype(BF), jnp.sum(grads, axis=0, keepdims=True)


def chip_swap(x):
    return lax.ppermute(x, "wid", CORE_PAIRS)


def body(activations, encoder, encoder_bias, decoder, decoder_bias, kept_mask, boundaries):
    tokens, width = activations.shape
    latents = encoder.shape[1]
    place = lax.axis_index("lat")
    core = lax.axis_index("wid") % N_CORE
    piece = width // SLICES
    span = lax.axis_size("lat") // GROUPS
    group = place // span
    y, z = place // N_Z, place % N_Z
    my_slice = NEAR * y + z % NEAR
    late = z // NEAR >= N_FAR // 2
    half = (tokens // N_CORE, latents)
    half_f32 = [(half, F32)] * 2
    half_low = [(half, BF)]
    many = [((N_X,) + half, BF)]
    sliced = [((SLICES, 2 * PIECE, tokens), BF)]

    has_cut = (place % span == 0) & (group > 0)
    cut = jnp.where(has_cut, boundaries[jnp.maximum(group - 1, 0)] - place * latents, 0)
    rows_act = activations.T
    dec_pad = pad_rows(decoder.T, piece).reshape(SLICES * PIECE, latents)
    target = lax.dynamic_index_in_dim(pad_rows(rows_act, piece), my_slice, 0, False).astype(F32)
    base = lax.dynamic_index_in_dim(pad_rows(decoder_bias[:, None], piece), my_slice, 0, False) - target

    kept, sent = call(encode, half_f32, [core], rows_act, encoder)
    (total,) = call(pair_sum, many, [core], kept, chip_swap(sent))
    pieces = swap(total, "wid", CHIP_GROUPS)
    (own_codes,) = call(kept_codes, half_low, [core], pieces, kept_mask, encoder_bias[None])
    other_codes = chip_swap(own_codes)

    (got,) = call(decode, sliced, [core, cut], own_codes, other_codes, dec_pad)
    got = swap(got, "lat", NEAR_GROUPS)
    (got,) = call(near_sums, [((N_FAR, N_Y, 2 * PIECE, tokens), BF)], [core], got)
    got = swap(got, "lat", FAR_GROUPS)
    (got,) = call(suffixes, sliced, [late, piece], got, base)
    got = swap(got, "lat", NEAR_GROUPS)

    kept, sent = call(back, half_f32, [core, cut], got, dec_pad)
    (total,) = call(pair_sum, many, [core], kept, chip_swap(sent))
    pieces = swap(total, "wid", CHIP_GROUPS)
    suffix_low = got[:, :piece].reshape(width, tokens)
    suffix_high = got[:, PIECE : PIECE + piece].reshape(width, tokens)
    low, high = split_codes(joined(core, own_codes, other_codes), cut)
    decoder_grad = (dot(suffix_low, low, (1, 0)) + dot(suffix_high, high, (1, 0))).astype(BF).T
    tags = got[:, piece : piece + 2, :piece].astype(F32)
    decoder_bias_grad = (tags[:, 0] + tags[:, 1]).reshape(width)
    (own_grads,) = call(kept_grads, half_low, [core], pieces, kept_mask)
    other_grads = chip_swap(own_grads)
    encoder_grad, encoder_bias_grad = call(
        encoder_grads, [((width, latents), BF), ((1, latents), F32)], [core], own_grads, other_grads, rows_act
    )
    return (encoder_grad, encoder_bias_grad.reshape(latents), decoder_grad, decoder_bias_grad)


def solution(mesh):
    placed = (
        P(None, "wid"),
        P("wid", "lat"),
        P("lat"),
        P("lat", "wid"),
        P("wid"),
        P(None, "lat"),
        P(),
    )
    return jax.shard_map(
        body,
        mesh=mesh,
        in_specs=placed,
        out_specs=(P("wid", "lat"), P("lat"), P("lat", "wid"), P("wid")),
        check_vma=False,
    )
```

```python
import jax
import jax.numpy as jnp
from jax import lax
from jax.experimental import pallas as pl
from jax.experimental.pallas import tpu as pltpu
from jax.sharding import PartitionSpec as P

GROUPS = 8
BF = jnp.bfloat16
F32 = jnp.float32

N_Y, N_FAR, NEAR = 4, 4, 4
N_Z = N_FAR * NEAR
SLICES = N_Y * NEAR
TURN = [0, 0, NEAR // 2, NEAR // 2]


def at(y, q, s):
    return N_Z * y + NEAR * q + (s + TURN[q]) % NEAR


NEAR_GROUPS = [[at(y, q, s) for y in range(N_Y) for s in range(NEAR)] for q in range(N_FAR)]
FAR_GROUPS = [[at(y, q, s) for q in range(N_FAR)] for y in range(N_Y) for s in range(NEAR)]
PIECE = 32
FILLED = 28
N_CORE, N_X = 2, 4
CORE_GROUPS = [[N_CORE * x + c for c in range(N_CORE)] for x in range(N_X)]
CHIP_GROUPS = [[N_CORE * x + c for x in range(N_X)] for c in range(N_CORE)]


def swap(x, axis, groups=None):
    return lax.all_to_all(x, axis, 0, 0, axis_index_groups=groups, tiled=False)


def copies(x, count):
    return jnp.broadcast_to(x[None], (count,) + x.shape)


def dot(a, b, over):
    return lax.dot_general(a, b, (((over[0],), (over[1],)), ((), ())), preferred_element_type=F32)


def to_slices(x):
    zeros = jnp.zeros((PIECE - FILLED, x.shape[1]), x.dtype)
    return jnp.stack([jnp.concatenate([x[FILLED * i : FILLED * (i + 1)], zeros], axis=0) for i in range(SLICES)])


def from_slices(x):
    return jnp.concatenate([x[i, :FILLED] for i in range(SLICES)], axis=0)


def call(stage, shapes, scalars, *arrays):
    n_in = len(arrays)
    scalars = scalars or [0]

    def kernel(scalar_ref, *refs):
        values = [scalar_ref[i] for i in range(len(scalars))]
        outs = stage(*values, *[ref[...] for ref in refs[:n_in]])
        for ref, out in zip(refs[n_in:], outs, strict=True):
            if isinstance(out, list):
                for i, one in enumerate(out):
                    ref[i] = one
            else:
                ref[...] = out

    vmem = pl.BlockSpec(memory_space=pltpu.VMEM)
    return pl.pallas_call(
        kernel,
        out_shape=[jax.ShapeDtypeStruct(shape, dtype) for shape, dtype in shapes],
        in_specs=[pl.BlockSpec(memory_space=pltpu.SMEM)] + [vmem] * n_in,
        out_specs=[vmem] * len(shapes),
        compiler_params=pltpu.CompilerParams(vmem_limit_bytes=32 * 1024 * 1024),
        name=stage.__name__,
    )(jnp.stack([jnp.asarray(v, jnp.int32) for v in scalars]), *arrays)


def half_of(core, x):
    half = x.shape[0] // N_CORE
    return jnp.where(core == 0, x[:half], x[half:])


def split_codes(codes, cut):
    below = lax.broadcasted_iota(jnp.int32, codes.shape, 1) < cut
    return jnp.where(below, codes, 0.0).astype(BF), jnp.where(below, 0.0, codes).astype(BF)


def encode_kernel(act_hbm, enc_hbm, out_ref, act, enc, sems):
    copies = [pltpu.make_async_copy(act_hbm, act, sems.at[0]), pltpu.make_async_copy(enc_hbm, enc, sems.at[1])]
    for copy in copies:
        copy.start()
    for copy in copies:
        copy.wait()
    out_ref[...] = dot(act[...], enc[...], (0, 0))


def encode(activations, encoder):
    hbm = pl.BlockSpec(memory_space=pltpu.HBM)
    return pl.pallas_call(
        encode_kernel,
        out_shape=jax.ShapeDtypeStruct((activations.shape[1], encoder.shape[1]), F32),
        in_specs=[hbm, hbm],
        out_specs=pl.BlockSpec(memory_space=pltpu.VMEM),
        scratch_shapes=[
            pltpu.VMEM(activations.shape, BF),
            pltpu.VMEM(encoder.shape, BF),
            pltpu.SemaphoreType.DMA((2,)),
        ],
        compiler_params=pltpu.CompilerParams(vmem_limit_bytes=32 * 1024 * 1024),
        name="encode",
    )(activations, encoder)


def pair_sum(core, parts):
    return ([(half_of(core, parts[0]) + half_of(core, parts[1])).astype(BF)] * N_X,)


def kept_codes(core, pieces, mask, bias):
    total = jnp.sum(pieces.astype(F32), axis=0) + bias
    return ((half_of(core, mask).astype(F32) * total).astype(BF),)


def kept_grads(core, pieces, mask):
    return ((half_of(core, mask).astype(F32) * jnp.sum(pieces.astype(F32), axis=0)).astype(BF),)


def lanes_of(core, x):
    zeros = jnp.zeros_like(x)
    first, second = jnp.concatenate([x, zeros], axis=0), jnp.concatenate([zeros, x], axis=0)
    return first if core == 0 else second


def decode(cut, codes, decoders):
    decoded = []
    for part in split_codes(codes.astype(F32), cut):
        both = dot(decoders[0], lanes_of(0, part), (1, 1)) + dot(decoders[1], lanes_of(1, part), (1, 1))
        decoded.append(to_slices(both))
    return (jnp.concatenate(decoded, axis=1).astype(BF),)


def near_sums(core, got):
    tokens = got.shape[-1]
    got = got.astype(F32).reshape(N_Y, NEAR, 2 * PIECE, tokens)
    return ([jnp.sum(got, axis=1).astype(BF)] * N_FAR,)


def suffixes(late, rows, got, base):
    got = got.astype(F32)
    low, high = got[:, :, :PIECE], got[:, :, PIECE:]
    run = base
    errors = []
    for y in range(N_Y):
        run = run + ((high[0, y] + high[1, y]) + low[2, y])
        errors.append(run)
        part = high[2, y] + high[3, y]
        run = run + (part + low[0, y + 1] if y + 1 < N_Y else part)
        errors.append(run)
    tail = jnp.zeros_like(base)
    suffix = []
    for error in reversed(errors):
        tail = tail + error
        suffix.append(tail / GROUPS)
    suffix = suffix[::-1]
    row = lax.broadcasted_iota(jnp.int32, base.shape, 0)
    lane = lax.broadcasted_iota(jnp.int32, base.shape, 1)
    tags = []
    own = lane < base.shape[1] // N_CORE
    for side in (own, jnp.logical_not(own)):
        token_sum = jnp.sum(jnp.where(side, suffix[0], 0.0), axis=1, keepdims=True)
        token_row = jnp.sum(jnp.where(row == lane, token_sum, 0.0), axis=0, keepdims=True)
        token_high = token_row.astype(BF).astype(F32)
        tags += [token_high, token_row - token_high]
    out = []
    for y in range(N_Y):
        own = jnp.where(late == 1, suffix[2 * y + 1], suffix[2 * y])
        previous = jnp.where(late == 1, suffix[2 * y], suffix[max(2 * y - 1, 0)])
        for i, tag in enumerate(tags):
            previous = jnp.where(row == rows + i, tag, previous)
        out += [jnp.concatenate([previous, own], axis=0).astype(BF)] * NEAR
    return (out,)


def slots(got):
    got = got.astype(F32)
    return from_slices(got[:, :PIECE]).astype(BF), from_slices(got[:, PIECE:]).astype(BF)


def back(cut, got, decoders):
    half = got.shape[-1] // N_CORE
    low, high = [dot(x, decoders[0], (0, 0))[:half] + dot(x, decoders[1], (0, 0))[half:] for x in slots(got)]
    below = lax.broadcasted_iota(jnp.int32, low.shape, 1) < cut
    return ([jnp.where(below, low, high).astype(BF)] * N_X,)


def decoder_grads(core, cut, got, codes):
    total = 0.0
    for half in range(N_CORE):
        parts = split_codes(codes[half].astype(F32), cut)
        for suffix, part in zip(slots(got[half]), parts):
            part = part.astype(F32)
            part = jnp.where(core == 0, lanes_of(0, part), lanes_of(1, part)).astype(BF)
            total = total + dot(suffix, part, (1, 0))
    return (total.astype(BF),)


def encoder_grads(_, grads, activations):
    grads = jnp.concatenate([grads[0], grads[1]], axis=0)
    bias = jnp.sum(grads.astype(F32), axis=0, keepdims=True)
    return dot(activations, grads, (1, 0)).astype(BF), bias


def both_cores(x):
    return lax.all_gather(x, "wid", axis_index_groups=CORE_GROUPS)


def body(activations, encoder, encoder_bias, decoder, decoder_bias, kept_mask, boundaries):
    tokens, width = activations.shape
    latents = encoder.shape[1]
    place = lax.axis_index("lat")
    core = lax.axis_index("wid") % N_CORE
    span = lax.axis_size("lat") // GROUPS
    group = place // span
    y, z = place // N_Z, place % N_Z
    late = z // NEAR >= N_FAR // 2
    my_slice = NEAR * y + (z - jnp.where(late, NEAR // 2, 0)) % NEAR
    half = (tokens // N_CORE, latents)
    half_low = [(half, BF)]
    many = [((N_X,) + half, BF)]
    sliced = [((SLICES, 2 * PIECE, tokens), BF)]

    has_cut = (place % span == 0) & (group > 0)
    cut = jnp.where(has_cut, boundaries[jnp.maximum(group - 1, 0)] - place * latents, 0)
    rows_act = activations.T

    (total,) = call(pair_sum, many, [core], both_cores(encode(rows_act, encoder)))
    decoder_rows, total = lax.optimization_barrier((decoder.T, total))
    pieces = swap(total, "wid", CHIP_GROUPS)
    decoders = both_cores(decoder_rows)
    (my_codes,) = call(kept_codes, half_low, [core], pieces, kept_mask, encoder_bias[None])

    target = lax.dynamic_index_in_dim(rows_act.reshape(SLICES, FILLED, tokens), my_slice, 0, False).astype(F32)
    base = lax.dynamic_index_in_dim(decoder_bias.reshape(SLICES, FILLED, 1), my_slice, 0, False) - target
    base = both_cores(jnp.pad(base, ((0, PIECE - FILLED), (0, 0))))
    base = jnp.where(core == 0, base[:, :, : half[0]], base[:, :, half[0] :])
    base = jnp.concatenate([base[0], base[1]], axis=1)

    (got,) = call(decode, sliced, [cut], my_codes, decoders)
    got = swap(got, "lat", NEAR_GROUPS)
    got, codes = lax.optimization_barrier((got, both_cores(my_codes)))
    (got,) = call(near_sums, [((N_FAR, N_Y, 2 * PIECE, tokens), BF)], [core], got)
    got = swap(got, "lat", FAR_GROUPS)
    (got,) = call(suffixes, sliced, [late, FILLED], got, base)
    got = swap(got, "lat", NEAR_GROUPS)

    (total,) = call(back, many, [cut], got, decoders)
    got, total = lax.optimization_barrier((got, total))
    pieces = swap(total, "wid", CHIP_GROUPS)
    got = both_cores(got)
    (decoder_grad,) = call(decoder_grads, [((width, latents), BF)], [core, cut], got, codes)
    first_tag = jnp.where(core == 0, FILLED, FILLED + 2)
    tags = lax.dynamic_slice_in_dim(got, first_tag, 2, 2)[..., :FILLED]
    decoder_bias_grad = jnp.sum(tags.astype(F32), axis=(0, 2)).reshape(width)
    (my_grads,) = call(kept_grads, half_low, [core], pieces, kept_mask)
    encoder_grad, encoder_bias_grad = call(
        encoder_grads, [((width, latents), BF), ((1, latents), F32)], [], both_cores(my_grads), rows_act
    )
    return (encoder_grad, encoder_bias_grad.reshape(latents), decoder_grad.T, decoder_bias_grad)


def solution(mesh):
    placed = (
        P(None, "wid"),
        P("wid", "lat"),
        P("lat"),
        P("lat", "wid"),
        P("wid"),
        P(None, "lat"),
        P(),
    )
    return jax.shard_map(
        body,
        mesh=mesh,
        in_specs=placed,
        out_specs=(P("wid", "lat"), P("lat"), P("lat", "wid"), P("wid")),
        check_vma=False,
    )
```

```python
import jax
import jax.numpy as jnp
from jax import lax
from jax.experimental import pallas as pl
from jax.experimental.pallas import tpu as pltpu
from jax.sharding import PartitionSpec as P

GROUPS = 8
BF = jnp.bfloat16
F32 = jnp.float32

N_Y, N_FAR, NEAR = 4, 4, 4
N_Z = N_FAR * NEAR
SLICES = N_Y * NEAR
TURN = [0, 0, NEAR // 2, NEAR // 2]


def at(y, q, s):
    return N_Z * y + NEAR * q + (s + TURN[q]) % NEAR


NEAR_GROUPS = [[at(y, q, s) for y in range(N_Y) for s in range(NEAR)] for q in range(N_FAR)]
FAR_GROUPS = [[at(y, q, s) for q in range(N_FAR)] for y in range(N_Y) for s in range(NEAR)]
PIECE = 28
ROWS = 2 * PIECE
TAG_ROWS = 8
N_CORE, N_X = 2, 4
CORE_GROUPS = [[N_CORE * x + c for c in range(N_CORE)] for x in range(N_X)]
CHIP_GROUPS = [[N_CORE * x + c for x in range(N_X)] for c in range(N_CORE)]


def swap(x, axis, groups=None):
    return lax.all_to_all(x, axis, 0, 0, axis_index_groups=groups, tiled=False)


def copies(x, count):
    return jnp.broadcast_to(x[None], (count,) + x.shape)


def dot(a, b, over):
    return lax.dot_general(a, b, (((over[0],), (over[1],)), ((), ())), preferred_element_type=F32)


def to_slices(first, second):
    rows = [[x[PIECE * i : PIECE * (i + 1)] for x in (first, second)] for i in range(SLICES)]
    return jnp.stack([jnp.concatenate(pair, axis=0) for pair in rows])


def from_slices(x, core):
    x = x.astype(F32)
    return jnp.concatenate([x[i, PIECE * core : PIECE * (core + 1)] for i in range(SLICES)], axis=0)


def call(stage, shapes, scalars, *arrays):
    n_in = len(arrays)
    scalars = scalars or [0]

    def kernel(scalar_ref, *refs):
        values = [scalar_ref[i] for i in range(len(scalars))]
        outs = stage(*values, *[ref[...] for ref in refs[:n_in]])
        for ref, out in zip(refs[n_in:], outs, strict=True):
            if isinstance(out, list):
                for i, one in enumerate(out):
                    ref[i] = one
            else:
                ref[...] = out

    vmem = pl.BlockSpec(memory_space=pltpu.VMEM)
    return pl.pallas_call(
        kernel,
        out_shape=[jax.ShapeDtypeStruct(shape, dtype) for shape, dtype in shapes],
        in_specs=[pl.BlockSpec(memory_space=pltpu.SMEM)] + [vmem] * n_in,
        out_specs=[vmem] * len(shapes),
        compiler_params=pltpu.CompilerParams(vmem_limit_bytes=32 * 1024 * 1024),
        name=stage.__name__,
    )(jnp.stack([jnp.asarray(v, jnp.int32) for v in scalars]), *arrays)


def half_of(core, x):
    half = x.shape[0] // N_CORE
    return jnp.where(core == 0, x[:half], x[half:])


def split_codes(codes, cut):
    codes = codes.astype(F32)
    below = lax.broadcasted_iota(jnp.int32, codes.shape, 1) < cut
    return jnp.concatenate([jnp.where(below, codes, 0.0), jnp.where(below, 0.0, codes)], axis=0).astype(BF)


def turned(_, activations):
    return (activations.astype(F32).T.astype(BF),)


def encode(_, activations, encoder):
    return (dot(activations, encoder, (1, 0)),)


def pair_sum(core, parts):
    return ([(half_of(core, parts[0]) + half_of(core, parts[1])).astype(BF)] * N_X,)


def kept_codes(core, pieces, mask, bias):
    total = jnp.sum(pieces.astype(F32), axis=0) + bias
    return ((half_of(core, mask).astype(F32) * total).astype(BF),)


def kept_grads(core, pieces, mask):
    return ((half_of(core, mask).astype(F32) * jnp.sum(pieces.astype(F32), axis=0)).astype(BF),)


def decode(cut, codes, decoders):
    codes = split_codes(codes, cut)
    first, second = [dot(decoders[core], codes, (1, 1)) for core in range(N_CORE)]
    return (to_slices(first, second).astype(BF),)


def near_sums(core, got):
    tokens = got.shape[-1]
    got = got.astype(F32).reshape(N_Y, NEAR, ROWS, tokens)
    return ([jnp.sum(got, axis=1).astype(BF)] * N_FAR,)


def suffixes(late, got, base):
    got = got.astype(F32)
    half = base.shape[1] // 2

    def other_half(x):
        return pltpu.roll(x, half, 1)

    run = base
    errors = []
    for y in range(N_Y):
        run = run + ((got[0, y] + got[1, y]) + other_half(got[2, y]))
        errors.append(run)
        part = got[2, y] + got[3, y]
        run = run + (part + other_half(got[0, y + 1]) if y + 1 < N_Y else part)
        errors.append(run)
    tail = jnp.zeros_like(base)
    suffix = []
    for error in reversed(errors):
        tail = tail + error
        suffix.append(tail / GROUPS)
    suffix = suffix[::-1]
    row = lax.broadcasted_iota(jnp.int32, base.shape, 0)
    lane = lax.broadcasted_iota(jnp.int32, base.shape, 1)
    token_sum = jnp.sum(jnp.where(lane < half, 0.0, suffix[0]), axis=1, keepdims=True)
    token_row = jnp.sum(jnp.where(row == lane, token_sum, 0.0), axis=0, keepdims=True)
    token_high = token_row.astype(BF).astype(F32)
    tag_row = lax.broadcasted_iota(jnp.int32, (TAG_ROWS, base.shape[1]), 0)
    tags = jnp.where(tag_row == 0, token_high, jnp.where(tag_row == 1, token_row - token_high, 0.0))
    out = []
    for y in range(N_Y):
        own = jnp.where(late == 1, suffix[2 * y + 1], suffix[2 * y])
        previous = jnp.where(late == 1, suffix[2 * y], suffix[max(2 * y - 1, 0)])
        pair = jnp.where(lane < half, other_half(previous), own)
        out += [jnp.concatenate([pair, tags], axis=0).astype(BF)] * NEAR
    return (out,)


def back(cut, got, decoders):
    parts = [dot(from_slices(got, core).astype(BF), decoders[core], (0, 0)) for core in range(N_CORE)]
    total = parts[0] + parts[1]
    half = total.shape[0] // 2
    below = lax.broadcasted_iota(jnp.int32, (half, total.shape[1]), 1) < cut
    return ([jnp.where(below, total[:half], total[half:]).astype(BF)] * N_X,)


def decoder_grads(core, cut, got, codes):
    total = 0.0
    for half in range(N_CORE):
        suffix = jnp.where(core == 0, from_slices(got[half], 0), from_slices(got[half], 1))
        total = total + dot(suffix.astype(BF), split_codes(codes[half], cut), (1, 0))
    return (total.astype(BF),)


def encoder_grads(_, grads, activations):
    grads = jnp.concatenate([grads[0], grads[1]], axis=0)
    bias = jnp.sum(grads.astype(F32), axis=0, keepdims=True)
    return dot(activations, grads, (1, 0)).astype(BF), bias


def both_cores(x):
    return lax.all_gather(x, "wid", axis_index_groups=CORE_GROUPS)


def body(activations, encoder, encoder_bias, decoder, decoder_bias, kept_mask, boundaries):
    tokens, width = activations.shape
    latents = encoder.shape[1]
    place = lax.axis_index("lat")
    core = lax.axis_index("wid") % N_CORE
    span = lax.axis_size("lat") // GROUPS
    group = place // span
    y, z = place // N_Z, place % N_Z
    late = z // NEAR >= N_FAR // 2
    my_slice = NEAR * y + (z - jnp.where(late, NEAR // 2, 0)) % NEAR
    half = (tokens // N_CORE, latents)
    half_low = [(half, BF)]
    many = [((N_X,) + half, BF)]

    has_cut = (place % span == 0) & (group > 0)
    cut = jnp.where(has_cut, boundaries[jnp.maximum(group - 1, 0)] - place * latents, 0)
    rows_act = activations.T

    (turned_act,) = call(turned, [((tokens, width), BF)], [], rows_act)
    (enc_part,) = call(encode, [((tokens, latents), F32)], [], turned_act, encoder)
    (total,) = call(pair_sum, many, [core], both_cores(enc_part))
    decoder_rows, total = lax.optimization_barrier((decoder.T, total))
    pieces = swap(total, "wid", CHIP_GROUPS)
    decoders = both_cores(decoder_rows)
    (my_codes,) = call(kept_codes, half_low, [core], pieces, kept_mask, encoder_bias[None])

    target = lax.dynamic_index_in_dim(rows_act.reshape(SLICES, PIECE, tokens), my_slice, 0, False).astype(F32)
    base = lax.dynamic_index_in_dim(decoder_bias.reshape(SLICES, PIECE, 1), my_slice, 0, False) - target
    base = both_cores(base).reshape(ROWS, tokens)
    base = jnp.where(core == 0, jnp.roll(base, half[0], axis=1), base)

    (got,) = call(decode, [((SLICES, ROWS, tokens), BF)], [cut], my_codes, decoders)
    got = swap(got, "lat", NEAR_GROUPS)
    (got,) = call(near_sums, [((N_FAR, N_Y, ROWS, tokens), BF)], [core], got)
    got = swap(got, "lat", FAR_GROUPS)
    got, codes = lax.optimization_barrier((got, both_cores(my_codes)))
    (got,) = call(suffixes, [((SLICES, ROWS + TAG_ROWS, tokens), BF)], [late], got, base)
    got = swap(got, "lat", NEAR_GROUPS)

    (total,) = call(back, many, [cut], got, decoders)
    got, total = lax.optimization_barrier((got, total))
    pieces = swap(total, "wid", CHIP_GROUPS)
    got = both_cores(got)
    (decoder_grad,) = call(decoder_grads, [((width, latents), BF)], [core, cut], got, codes)
    tags = lax.dynamic_slice_in_dim(got[:, :, ROWS : ROWS + 2], core * PIECE, PIECE, 3)
    decoder_bias_grad = jnp.sum(tags.astype(F32), axis=(0, 2)).reshape(width)
    (my_grads,) = call(kept_grads, half_low, [core], pieces, kept_mask)
    encoder_grad, encoder_bias_grad = call(
        encoder_grads, [((width, latents), BF), ((1, latents), F32)], [], both_cores(my_grads), rows_act
    )
    return (encoder_grad, encoder_bias_grad.reshape(latents), decoder_grad.T, decoder_bias_grad)


def solution(mesh):
    placed = (
        P(None, "wid"),
        P("wid", "lat"),
        P("lat"),
        P("lat", "wid"),
        P("wid"),
        P(None, "lat"),
        P(),
    )
    return jax.shard_map(
        body,
        mesh=mesh,
        in_specs=placed,
        out_specs=(P("wid", "lat"), P("lat"), P("lat", "wid"), P("wid")),
        check_vma=False,
    )
```

```python
import collections

import jax
import jax.numpy as jnp
from jax import lax
from jax.experimental import pallas as pl
from jax.experimental.pallas import tpu as pltpu
from jax.sharding import PartitionSpec as P

GROUPS = 8
BF = jnp.bfloat16
F32 = jnp.float32

N_Y, N_FAR, NEAR = 4, 4, 4
N_Z = N_FAR * NEAR
SLICES = N_Y * NEAR
TURN = [0, 0, NEAR // 2, NEAR // 2]


def at(y, q, s):
    return N_Z * y + NEAR * q + (s + TURN[q]) % NEAR


NEAR_GROUPS = [[at(y, q, s) for y in range(N_Y) for s in range(NEAR)] for q in range(N_FAR)]
FAR_GROUPS = [[at(y, q, s) for q in range(N_FAR)] for y in range(N_Y) for s in range(NEAR)]
PIECE = 28
ROWS = 2 * PIECE
TAG_ROWS = 8
N_CORE, N_X = 2, 4
CORE_GROUPS = [[N_CORE * x + c for c in range(N_CORE)] for x in range(N_X)]
CHIP_GROUPS = [[N_CORE * x + c for x in range(N_X)] for c in range(N_CORE)]


Scalars = collections.namedtuple('Scalars', ['core', 'late', 'cut', 'my_slice'], defaults=(None, None, None))


def swap(x, axis, groups=None):
    return lax.all_to_all(x, axis, 0, 0, axis_index_groups=groups, tiled=False)


def copies(x, count):
    return jnp.broadcast_to(x[None], (count,) + x.shape)


def dot(a, b, over):
    return lax.dot_general(a, b, (((over[0],), (over[1],)), ((), ())), preferred_element_type=F32)


def to_slices(first, second):
    rows = [[x[PIECE * i : PIECE * (i + 1)] for x in (first, second)] for i in range(SLICES)]
    return jnp.stack([jnp.concatenate(pair, axis=0) for pair in rows])


def from_slices(x, core):
    x = x.astype(F32)
    return jnp.concatenate([x[i, PIECE * core : PIECE * (core + 1)] for i in range(SLICES)], axis=0)


def call(stage, shapes, scalars, *arrays):
    n_in = len(arrays)

    def kernel(scalar_ref, *refs):
        at = Scalars(*[scalar_ref[i] for i in range(scalars.shape[0])])
        outs = stage(at, *[ref[...] for ref in refs[:n_in]])
        for ref, out in zip(refs[n_in:], outs, strict=True):
            if isinstance(out, list):
                for i, one in enumerate(out):
                    ref[i] = one
            else:
                ref[...] = out

    vmem = pl.BlockSpec(memory_space=pltpu.VMEM)
    return pl.pallas_call(
        kernel,
        out_shape=[jax.ShapeDtypeStruct(shape, dtype) for shape, dtype in shapes],
        in_specs=[pl.BlockSpec(memory_space=pltpu.SMEM)] + [vmem] * n_in,
        out_specs=[vmem] * len(shapes),
        compiler_params=pltpu.CompilerParams(vmem_limit_bytes=32 * 1024 * 1024),
        name=stage.__name__,
    )(scalars, *arrays)


def half_of(core, x):
    half = x.shape[0] // N_CORE
    return jnp.where(core == 0, x[:half], x[half:])


def split_codes(codes, cut):
    codes = codes.astype(F32)
    below = lax.broadcasted_iota(jnp.int32, codes.shape, 1) < cut
    return jnp.concatenate([jnp.where(below, codes, 0.0), jnp.where(below, 0.0, codes)], axis=0).astype(BF)


def encode_kernel(act_hbm, enc_hbm, out_ref, act, enc, sems):
    copies = [pltpu.make_async_copy(act_hbm, act, sems.at[0]), pltpu.make_async_copy(enc_hbm, enc, sems.at[1])]
    for copy in copies:
        copy.start()
    for copy in copies:
        copy.wait()
    out_ref[...] = dot(act[...], enc[...], (0, 0))


def encode(activations, encoder):
    hbm = pl.BlockSpec(memory_space=pltpu.HBM)
    return pl.pallas_call(
        encode_kernel,
        out_shape=jax.ShapeDtypeStruct((activations.shape[1], encoder.shape[1]), F32),
        in_specs=[hbm, hbm],
        out_specs=pl.BlockSpec(memory_space=pltpu.VMEM),
        scratch_shapes=[
            pltpu.VMEM(activations.shape, BF),
            pltpu.VMEM(encoder.shape, BF),
            pltpu.SemaphoreType.DMA((2,)),
        ],
        compiler_params=pltpu.CompilerParams(vmem_limit_bytes=56 * 1024 * 1024),
        name="encode",
    )(activations, encoder)


def pair_sum(at, parts):
    return ([(half_of(at.core, parts[0]) + half_of(at.core, parts[1])).astype(BF)] * N_X,)


def kept_codes(at, pieces, mask, bias):
    total = jnp.sum(pieces.astype(F32), axis=0) + bias
    return ((half_of(at.core, mask).astype(F32) * total).astype(BF),)


def kept_grads(at, pieces, mask):
    return ((half_of(at.core, mask).astype(F32) * jnp.sum(pieces.astype(F32), axis=0)).astype(BF),)


def decode(at, codes, decoders):
    codes = split_codes(codes, at.cut)
    first, second = [dot(decoders[core], codes, (1, 1)) for core in range(N_CORE)]
    return (to_slices(first, second).astype(BF),)


def near_sums(_, got):
    tokens = got.shape[-1]
    got = got.astype(F32).reshape(N_Y, NEAR, ROWS, tokens)
    return ([jnp.sum(got, axis=1).astype(BF)] * N_FAR,)


def own_base(at, activations, bias):
    base = bias - activations.astype(F32)
    pieces = [jnp.where(at.my_slice == i, base[PIECE * i : PIECE * (i + 1)], 0.0) for i in range(SLICES)]
    return (sum(pieces),)


def suffixes(at, got, bases):
    got = got.astype(F32)
    base = jnp.concatenate([bases[0], bases[1]], axis=0)
    half = base.shape[1] // 2

    def other_half(x):
        return pltpu.roll(x, half, 1)

    base = jnp.where(at.core == 0, other_half(base), base)
    run = base
    errors = []
    for y in range(N_Y):
        run = run + ((got[0, y] + got[1, y]) + other_half(got[2, y]))
        errors.append(run)
        part = got[2, y] + got[3, y]
        run = run + (part + other_half(got[0, y + 1]) if y + 1 < N_Y else part)
        errors.append(run)
    tail = jnp.zeros_like(base)
    suffix = []
    for error in reversed(errors):
        tail = tail + error
        suffix.append(tail / GROUPS)
    suffix = suffix[::-1]
    row = lax.broadcasted_iota(jnp.int32, base.shape, 0)
    lane = lax.broadcasted_iota(jnp.int32, base.shape, 1)
    token_sum = jnp.sum(jnp.where(lane < half, 0.0, suffix[0]), axis=1, keepdims=True)
    token_row = jnp.sum(jnp.where(row == lane, token_sum, 0.0), axis=0, keepdims=True)
    token_high = token_row.astype(BF).astype(F32)
    tag_row = lax.broadcasted_iota(jnp.int32, (TAG_ROWS, base.shape[1]), 0)
    tags = jnp.where(tag_row == 0, token_high, jnp.where(tag_row == 1, token_row - token_high, 0.0))
    out = []
    for y in range(N_Y):
        own = jnp.where(at.late == 1, suffix[2 * y + 1], suffix[2 * y])
        previous = jnp.where(at.late == 1, suffix[2 * y], suffix[max(2 * y - 1, 0)])
        pair = jnp.where(lane < half, other_half(previous), own)
        out += [jnp.concatenate([pair, tags], axis=0).astype(BF)] * NEAR
    return (out,)


def back(at, got, decoders):
    parts = [dot(from_slices(got, core).astype(BF), decoders[core], (0, 0)) for core in range(N_CORE)]
    total = parts[0] + parts[1]
    half = total.shape[0] // 2
    below = lax.broadcasted_iota(jnp.int32, (half, total.shape[1]), 1) < at.cut
    return ([jnp.where(below, total[:half], total[half:]).astype(BF)] * N_X,)


def decoder_grads(at, got, codes):
    total, tags = 0.0, 0.0
    for half in range(N_CORE):
        suffix = jnp.where(at.core == 0, from_slices(got[half], 0), from_slices(got[half], 1))
        total = total + dot(suffix.astype(BF), split_codes(codes[half], at.cut), (1, 0))
        tags = tags + jnp.sum(got[half, :, ROWS:].astype(F32), axis=1)
    tags = jnp.where(at.core == 0, tags, pltpu.roll(tags, tags.shape[1] - PIECE, 1))
    return total.astype(BF), tags


def encoder_grads(_, grads, activations):
    grads = jnp.concatenate([grads[0], grads[1]], axis=0)
    bias = jnp.sum(grads.astype(F32), axis=0, keepdims=True)
    return dot(activations, grads, (1, 0)).astype(BF), bias


def both_cores(x):
    return lax.all_gather(x, "wid", axis_index_groups=CORE_GROUPS)


def body(activations, encoder, encoder_bias, decoder, decoder_bias, kept_mask, boundaries):
    tokens, width = activations.shape
    latents = encoder.shape[1]
    place = lax.axis_index("lat")
    core = lax.axis_index("wid") % N_CORE
    span = lax.axis_size("lat") // GROUPS
    group = place // span
    y, z = place // N_Z, place % N_Z
    late = z // NEAR >= N_FAR // 2
    my_slice = NEAR * y + (z - jnp.where(late, NEAR // 2, 0)) % NEAR
    half = (tokens // N_CORE, latents)
    half_low = [(half, BF)]
    many = [((N_X,) + half, BF)]
    rows_act = activations.T

    (total,) = call(pair_sum, many, core.reshape(1), both_cores(encode(rows_act, encoder)))
    decoder_rows, boundaries, total = lax.optimization_barrier((decoder.T, boundaries, total))

    has_cut = (place % span == 0) & (group > 0)
    cut = jnp.where(has_cut, boundaries[jnp.maximum(group - 1, 0)] - place * latents, 0)
    at = jnp.stack(Scalars(core, late.astype(jnp.int32), cut, my_slice))

    pieces = swap(total, "wid", CHIP_GROUPS)
    decoders = both_cores(decoder_rows)
    (my_codes,) = call(kept_codes, half_low, at, pieces, kept_mask, encoder_bias[None])

    (got,) = call(decode, [((SLICES, ROWS, tokens), BF)], at, my_codes, decoders)
    got = swap(got, "lat", NEAR_GROUPS)
    (got,) = call(near_sums, [((N_FAR, N_Y, ROWS, tokens), BF)], at, got)
    later_act, later_bias, later_codes, got = lax.optimization_barrier((rows_act, decoder_bias, my_codes, got))
    got = swap(got, "lat", FAR_GROUPS)
    (base,) = call(own_base, [((PIECE, tokens), F32)], at, later_act, later_bias[:, None])
    base, codes = both_cores(base), both_cores(later_codes)
    got, base, codes = lax.optimization_barrier((got, base, codes))
    (got,) = call(suffixes, [((SLICES, ROWS + TAG_ROWS, tokens), BF)], at, got, base)
    got = swap(got, "lat", NEAR_GROUPS)

    (total,) = call(back, many, at, got, decoders)
    got, total = lax.optimization_barrier((got, total))
    pieces = swap(total, "wid", CHIP_GROUPS)
    decoder_grad, tags = call(
        decoder_grads, [((width, latents), BF), ((SLICES, tokens), F32)], at, both_cores(got), codes
    )
    decoder_bias_grad = tags[:, :PIECE].reshape(width)
    (my_grads,) = call(kept_grads, half_low, at, pieces, kept_mask)
    encoder_grad, encoder_bias_grad = call(
        encoder_grads, [((width, latents), BF), ((1, latents), F32)], at, both_cores(my_grads), rows_act
    )
    return (encoder_grad, encoder_bias_grad.reshape(latents), decoder_grad.T, decoder_bias_grad)


def solution(mesh):
    placed = (
        P(None, "wid"),
        P("wid", "lat"),
        P("lat"),
        P("lat", "wid"),
        P("wid"),
        P(None, "lat"),
        P(),
    )
    return jax.shard_map(
        body,
        mesh=mesh,
        in_specs=placed,
        out_specs=(P("wid", "lat"), P("lat"), P("lat", "wid"), P("wid")),
        check_vma=False,
    )
```

```python
import collections

import jax
import jax.numpy as jnp
from jax import lax
from jax.experimental import pallas as pl
from jax.experimental.pallas import tpu as pltpu
from jax.sharding import PartitionSpec as P

GROUPS = 8
BF = jnp.bfloat16
F32 = jnp.float32

N_Y, N_FAR, NEAR = 4, 4, 4
N_Z = N_FAR * NEAR
SLICES = N_Y * NEAR
TURN = [0, 0, NEAR // 2, NEAR // 2]


def at(y, q, s):
    return N_Z * y + NEAR * q + (s + TURN[q]) % NEAR


NEAR_GROUPS = [[at(y, q, s) for y in range(N_Y) for s in range(NEAR)] for q in range(N_FAR)]
FAR_GROUPS = [[at(y, q, s) for q in range(N_FAR)] for y in range(N_Y) for s in range(NEAR)]
PIECE = 28
ROWS = 2 * PIECE
TAG_ROWS = 8
N_CORE, N_X = 2, 4
CORE_GROUPS = [[N_CORE * x + c for c in range(N_CORE)] for x in range(N_X)]
CHIP_GROUPS = [[N_CORE * x + c for x in range(N_X)] for c in range(N_CORE)]


Scalars = collections.namedtuple('Scalars', ['core', 'late', 'cut', 'my_slice'], defaults=(None,) * 4)


def swap(x, axis, groups=None):
    return lax.all_to_all(x, axis, 0, 0, axis_index_groups=groups, tiled=False)


def copies(x, count):
    return jnp.broadcast_to(x[None], (count,) + x.shape)


def dot(a, b, over):
    return lax.dot_general(a, b, (((over[0],), (over[1],)), ((), ())), preferred_element_type=F32)


def to_slices(first, second):
    rows = [[x[PIECE * i : PIECE * (i + 1)] for x in (first, second)] for i in range(SLICES)]
    return jnp.stack([jnp.concatenate(pair, axis=0) for pair in rows])


def from_slices(x, core):
    x = x.astype(F32)
    return jnp.concatenate([x[i, PIECE * core : PIECE * (core + 1)] for i in range(SLICES)], axis=0)


def call(stage, shapes, scalars, *arrays):
    names = list(scalars)
    n_out = len(shapes)

    def kernel(*refs):
        at = Scalars(**{name: ref[0] for name, ref in zip(names, refs)})
        outs = stage(at, *[ref[...] for ref in refs[len(names) : -n_out]])
        for ref, out in zip(refs[-n_out:], outs, strict=True):
            if isinstance(out, list):
                for i, one in enumerate(out):
                    ref[i] = one
            else:
                ref[...] = out

    vmem = pl.BlockSpec(memory_space=pltpu.VMEM)
    return pl.pallas_call(
        kernel,
        out_shape=[jax.ShapeDtypeStruct(shape, dtype) for shape, dtype in shapes],
        in_specs=[pl.BlockSpec(memory_space=pltpu.SMEM)] * len(names) + [vmem] * len(arrays),
        out_specs=[vmem] * n_out,
        compiler_params=pltpu.CompilerParams(vmem_limit_bytes=32 * 1024 * 1024),
        name=stage.__name__,
    )(*[scalars[name].reshape(1) for name in names], *arrays)


def half_of(core, x):
    half = x.shape[0] // N_CORE
    return jnp.where(core == 0, x[:half], x[half:])


def split_codes(codes, cut):
    codes = codes.astype(F32)
    below = lax.broadcasted_iota(jnp.int32, codes.shape, 1) < cut
    return jnp.concatenate([jnp.where(below, codes, 0.0), jnp.where(below, 0.0, codes)], axis=0).astype(BF)


def encode(_, activations, encoder):
    return (dot(activations, encoder, (0, 0)),)


def pair_sum(at, parts):
    return ([(half_of(at.core, parts[0]) + half_of(at.core, parts[1])).astype(BF)] * N_X,)


def kept_codes(at, pieces, mask, bias):
    total = jnp.sum(pieces.astype(F32), axis=0) + bias
    return ((half_of(at.core, mask).astype(F32) * total).astype(BF),)


def kept_grads(at, pieces, mask):
    return ((half_of(at.core, mask).astype(F32) * jnp.sum(pieces.astype(F32), axis=0)).astype(BF),)


def decode(at, codes, decoders):
    codes = split_codes(codes, at.cut)
    first, second = [dot(decoders[core], codes, (1, 1)) for core in range(N_CORE)]
    return (to_slices(first, second).astype(BF),)


def near_sums(_, got):
    tokens = got.shape[-1]
    got = got.astype(F32).reshape(N_Y, NEAR, ROWS, tokens)
    return ([jnp.sum(got, axis=1).astype(BF)] * N_FAR,)


def own_base(at, activations, bias):
    base = bias - activations.astype(F32)
    pieces = [jnp.where(at.my_slice == i, base[PIECE * i : PIECE * (i + 1)], 0.0) for i in range(SLICES)]
    return (sum(pieces),)


def suffixes(at, got, bases):
    got = got.astype(F32)
    base = jnp.concatenate([bases[0], bases[1]], axis=0)
    half = base.shape[1] // 2

    def other_half(x):
        return pltpu.roll(x, half, 1)

    base = jnp.where(at.core == 0, other_half(base), base)
    run = base
    errors = []
    for y in range(N_Y):
        run = run + ((got[0, y] + got[1, y]) + other_half(got[2, y]))
        errors.append(run)
        part = got[2, y] + got[3, y]
        run = run + (part + other_half(got[0, y + 1]) if y + 1 < N_Y else part)
        errors.append(run)
    tail = jnp.zeros_like(base)
    suffix = []
    for error in reversed(errors):
        tail = tail + error
        suffix.append(tail / GROUPS)
    suffix = suffix[::-1]
    row = lax.broadcasted_iota(jnp.int32, base.shape, 0)
    lane = lax.broadcasted_iota(jnp.int32, base.shape, 1)
    token_sum = jnp.sum(jnp.where(lane < half, 0.0, suffix[0]), axis=1, keepdims=True)
    token_row = jnp.sum(jnp.where(row == lane, token_sum, 0.0), axis=0, keepdims=True)
    token_high = token_row.astype(BF).astype(F32)
    tag_row = lax.broadcasted_iota(jnp.int32, (TAG_ROWS, base.shape[1]), 0)
    tags = jnp.where(tag_row == 0, token_high, jnp.where(tag_row == 1, token_row - token_high, 0.0))
    out = []
    for y in range(N_Y):
        own = jnp.where(at.late == 1, suffix[2 * y + 1], suffix[2 * y])
        previous = jnp.where(at.late == 1, suffix[2 * y], suffix[max(2 * y - 1, 0)])
        pair = jnp.where(lane < half, other_half(previous), own)
        out += [jnp.concatenate([pair, tags], axis=0).astype(BF)] * NEAR
    return (out,)


def back(at, got, decoders):
    parts = [dot(from_slices(got, core).astype(BF), decoders[core], (0, 0)) for core in range(N_CORE)]
    total = parts[0] + parts[1]
    half = total.shape[0] // 2
    below = lax.broadcasted_iota(jnp.int32, (half, total.shape[1]), 1) < at.cut
    return ([jnp.where(below, total[:half], total[half:]).astype(BF)] * N_X,)


def decoder_grads(at, got, codes):
    total, tags = 0.0, 0.0
    for half in range(N_CORE):
        suffix = jnp.where(at.core == 0, from_slices(got[half], 0), from_slices(got[half], 1))
        total = total + dot(suffix.astype(BF), split_codes(codes[half], at.cut), (1, 0))
        tags = tags + jnp.sum(got[half, :, ROWS:].astype(F32), axis=1)
    tags = jnp.where(at.core == 0, tags, pltpu.roll(tags, tags.shape[1] - PIECE, 1))
    return total.astype(BF), tags


def encoder_grads(_, grads, activations):
    grads = jnp.concatenate([grads[0], grads[1]], axis=0)
    bias = jnp.sum(grads.astype(F32), axis=0, keepdims=True)
    return dot(activations, grads, (1, 0)).astype(BF), bias


def both_cores(x):
    return lax.all_gather(x, "wid", axis_index_groups=CORE_GROUPS)


def body(activations, encoder, encoder_bias, decoder, decoder_bias, kept_mask, boundaries):
    tokens, width = activations.shape
    latents = encoder.shape[1]
    place = lax.axis_index("lat")
    core = lax.axis_index("wid") % N_CORE
    span = lax.axis_size("lat") // GROUPS
    group = place // span
    y, z = place // N_Z, place % N_Z
    late = z // NEAR >= N_FAR // 2
    my_slice = NEAR * y + (z - jnp.where(late, NEAR // 2, 0)) % NEAR
    half = (tokens // N_CORE, latents)
    half_low = [(half, BF)]
    many = [((N_X,) + half, BF)]
    rows_act = activations.T

    on_core = {'core': core}
    (enc_part,) = call(encode, [((tokens, latents), F32)], {}, rows_act, encoder)
    (total,) = call(pair_sum, many, on_core, both_cores(enc_part))
    decoder_rows, boundaries, total = lax.optimization_barrier((decoder.T, boundaries, total))

    has_cut = (place % span == 0) & (group > 0)
    cut = jnp.where(has_cut, boundaries[jnp.maximum(group - 1, 0)] - place * latents, 0)
    late = late.astype(jnp.int32)
    at_cut = {'cut': cut}

    pieces = swap(total, "wid", CHIP_GROUPS)
    decoders = both_cores(decoder_rows)
    (my_codes,) = call(kept_codes, half_low, on_core, pieces, kept_mask, encoder_bias[None])

    (got,) = call(decode, [((SLICES, ROWS, tokens), BF)], at_cut, my_codes, decoders)
    got = swap(got, "lat", NEAR_GROUPS)
    (got,) = call(near_sums, [((N_FAR, N_Y, ROWS, tokens), BF)], {}, got)
    later_act, later_bias, later_codes, got = lax.optimization_barrier((rows_act, decoder_bias, my_codes, got))
    got = swap(got, "lat", FAR_GROUPS)
    (base,) = call(own_base, [((PIECE, tokens), F32)], {'my_slice': my_slice}, later_act, later_bias[:, None])
    base, codes = both_cores(base), both_cores(later_codes)
    got, base, codes = lax.optimization_barrier((got, base, codes))
    (got,) = call(suffixes, [((SLICES, ROWS + TAG_ROWS, tokens), BF)], {'core': core, 'late': late}, got, base)
    got = swap(got, "lat", NEAR_GROUPS)

    (total,) = call(back, many, at_cut, got, decoders)
    got, total = lax.optimization_barrier((got, total))
    pieces = swap(total, "wid", CHIP_GROUPS)
    decoder_grad, tags = call(
        decoder_grads, [((width, latents), BF), ((SLICES, tokens), F32)], {'core': core, 'cut': cut}, both_cores(got), codes
    )
    decoder_bias_grad = tags[:, :PIECE].reshape(width)
    (my_grads,) = call(kept_grads, half_low, on_core, pieces, kept_mask)
    encoder_grad, encoder_bias_grad = call(
        encoder_grads, [((width, latents), BF), ((1, latents), F32)], {}, both_cores(my_grads), rows_act
    )
    return (encoder_grad, encoder_bias_grad.reshape(latents), decoder_grad.T, decoder_bias_grad)


def solution(mesh):
    placed = (
        P(None, "wid"),
        P("wid", "lat"),
        P("lat"),
        P("lat", "wid"),
        P("wid"),
        P(None, "lat"),
        P(),
    )
    return jax.shard_map(
        body,
        mesh=mesh,
        in_specs=placed,
        out_specs=(P("wid", "lat"), P("lat"), P("lat", "wid"), P("wid")),
        check_vma=False,
    )
```

```python
import collections

import jax
import jax.numpy as jnp
from jax import lax
from jax.experimental import pallas as pl
from jax.experimental.pallas import tpu as pltpu
from jax.sharding import PartitionSpec as P

GROUPS = 8
BF = jnp.bfloat16
F32 = jnp.float32

N_Y, N_FAR, NEAR = 4, 4, 4
N_Z = N_FAR * NEAR
SLICES = N_Y * NEAR
TURN = [0, 0, NEAR // 2, NEAR // 2]


def at(y, q, s):
    return N_Z * y + NEAR * q + (s + TURN[q]) % NEAR


NEAR_GROUPS = [[at(y, q, s) for y in range(N_Y) for s in range(NEAR)] for q in range(N_FAR)]
FAR_GROUPS = [[at(y, q, s) for q in range(N_FAR)] for y in range(N_Y) for s in range(NEAR)]
PIECE = 28
ROWS = 2 * PIECE
TAG_ROWS = 8
N_CORE, N_X = 2, 4
CORE_GROUPS = [[N_CORE * x + c for c in range(N_CORE)] for x in range(N_X)]
CHIP_GROUPS = [[N_CORE * x + c for x in range(N_X)] for c in range(N_CORE)]


Scalars = collections.namedtuple('Scalars', ['core', 'late', 'cut', 'my_slice'], defaults=(None,) * 4)


def swap(x, axis, groups=None):
    return lax.all_to_all(x, axis, 0, 0, axis_index_groups=groups, tiled=False)


def copies(x, count):
    return jnp.broadcast_to(x[None], (count,) + x.shape)


def dot(a, b, over):
    return lax.dot_general(a, b, (((over[0],), (over[1],)), ((), ())), preferred_element_type=F32)


def to_slices(first, second):
    rows = [[x[PIECE * i : PIECE * (i + 1)] for x in (first, second)] for i in range(SLICES)]
    return jnp.stack([jnp.concatenate(pair, axis=0) for pair in rows])


def from_slices(x, core):
    x = x.astype(F32)
    return jnp.concatenate([x[i, PIECE * core : PIECE * (core + 1)] for i in range(SLICES)], axis=0)


def call(stage, shapes, scalars, *arrays):
    names = list(scalars)
    n_out = len(shapes)

    def kernel(*refs):
        at = Scalars(**{name: ref[0] for name, ref in zip(names, refs)})
        outs = stage(at, *[ref[...] for ref in refs[len(names) : -n_out]])
        for ref, out in zip(refs[-n_out:], outs, strict=True):
            if isinstance(out, list):
                for i, one in enumerate(out):
                    ref[i] = one
            else:
                ref[...] = out

    vmem = pl.BlockSpec(memory_space=pltpu.VMEM)
    return pl.pallas_call(
        kernel,
        out_shape=[jax.ShapeDtypeStruct(shape, dtype) for shape, dtype in shapes],
        in_specs=[pl.BlockSpec(memory_space=pltpu.SMEM)] * len(names) + [vmem] * len(arrays),
        out_specs=[vmem] * n_out,
        compiler_params=pltpu.CompilerParams(vmem_limit_bytes=32 * 1024 * 1024),
        name=stage.__name__,
    )(*[scalars[name].reshape(1) for name in names], *arrays)


def half_of(core, x):
    half = x.shape[0] // N_CORE
    return jnp.where(core == 0, x[:half], x[half:])


def split_codes(codes, cut):
    codes = codes.astype(F32)
    below = lax.broadcasted_iota(jnp.int32, codes.shape, 1) < cut
    return jnp.concatenate([jnp.where(below, codes, 0.0), jnp.where(below, 0.0, codes)], axis=0).astype(BF)


def lanes_of(core, x):
    half = x.shape[1] // N_CORE
    return jnp.where(core == 0, x[:, :half], x[:, half:])


def encode(at, sides, activations):
    half = activations.shape[1] // N_CORE
    latents = sides.shape[2] - half
    mine = lanes_of(at.core, activations.astype(F32))
    part = 0.0
    for core in range(N_CORE):
        theirs = sides[core, :, latents:].astype(F32)
        rows = jnp.where(at.core == core, mine, theirs).astype(BF)
        part = part + dot(rows, sides[core, :, :latents], (0, 0))
    return ([part.astype(BF)] * N_X,)


def kept_codes(at, pieces, mask, bias):
    total = jnp.sum(pieces.astype(F32), axis=0) + bias
    return ((half_of(at.core, mask).astype(F32) * total).astype(BF),)


def kept_grads(at, pieces, mask):
    return ((half_of(at.core, mask).astype(F32) * jnp.sum(pieces.astype(F32), axis=0)).astype(BF),)


def decode(at, codes, decoders):
    codes = split_codes(codes, at.cut)
    first, second = [dot(decoders[core], codes, (1, 1)) for core in range(N_CORE)]
    return (to_slices(first, second).astype(BF),)


def near_sums(_, got):
    tokens = got.shape[-1]
    got = got.astype(F32).reshape(N_Y, NEAR, ROWS, tokens)
    return ([jnp.sum(got, axis=1).astype(BF)] * N_FAR,)


def own_base(at, activations, bias):
    base = bias - activations.astype(F32)
    pieces = [jnp.where(at.my_slice == i, base[PIECE * i : PIECE * (i + 1)], 0.0) for i in range(SLICES)]
    return (sum(pieces),)


def suffixes(at, got, bases):
    got = got.astype(F32)
    base = jnp.concatenate([bases[0], bases[1]], axis=0)
    half = base.shape[1] // 2

    def other_half(x):
        return pltpu.roll(x, half, 1)

    base = jnp.where(at.core == 0, other_half(base), base)
    run = base
    errors = []
    for y in range(N_Y):
        run = run + ((got[0, y] + got[1, y]) + other_half(got[2, y]))
        errors.append(run)
        part = got[2, y] + got[3, y]
        run = run + (part + other_half(got[0, y + 1]) if y + 1 < N_Y else part)
        errors.append(run)
    tail = jnp.zeros_like(base)
    suffix = []
    for error in reversed(errors):
        tail = tail + error
        suffix.append(tail / GROUPS)
    suffix = suffix[::-1]
    row = lax.broadcasted_iota(jnp.int32, base.shape, 0)
    lane = lax.broadcasted_iota(jnp.int32, base.shape, 1)
    token_sum = jnp.sum(jnp.where(lane < half, 0.0, suffix[0]), axis=1, keepdims=True)
    token_row = jnp.sum(jnp.where(row == lane, token_sum, 0.0), axis=0, keepdims=True)
    token_high = token_row.astype(BF).astype(F32)
    tag_row = lax.broadcasted_iota(jnp.int32, (TAG_ROWS, base.shape[1]), 0)
    tags = jnp.where(tag_row == 0, token_high, jnp.where(tag_row == 1, token_row - token_high, 0.0))
    out = []
    for y in range(N_Y):
        own = jnp.where(at.late == 1, suffix[2 * y + 1], suffix[2 * y])
        previous = jnp.where(at.late == 1, suffix[2 * y], suffix[max(2 * y - 1, 0)])
        pair = jnp.where(lane < half, other_half(previous), own)
        out += [jnp.concatenate([pair, tags], axis=0).astype(BF)] * NEAR
    return (out,)


def back(at, got, decoders):
    parts = [dot(from_slices(got, core).astype(BF), decoders[core], (0, 0)) for core in range(N_CORE)]
    total = parts[0] + parts[1]
    half = total.shape[0] // 2
    below = lax.broadcasted_iota(jnp.int32, (half, total.shape[1]), 1) < at.cut
    return ([jnp.where(below, total[:half], total[half:]).astype(BF)] * N_X,)


def decoder_grads(at, got, codes):
    total, tags = 0.0, 0.0
    for half in range(N_CORE):
        suffix = jnp.where(at.core == 0, from_slices(got[half], 0), from_slices(got[half], 1))
        total = total + dot(suffix.astype(BF), split_codes(codes[half], at.cut), (1, 0))
        tags = tags + jnp.sum(got[half, :, ROWS:].astype(F32), axis=1)
    tags = jnp.where(at.core == 0, tags, pltpu.roll(tags, tags.shape[1] - PIECE, 1))
    return total.astype(BF), tags


def encoder_grads(_, grads, activations):
    grads = jnp.concatenate([grads[0], grads[1]], axis=0)
    bias = jnp.sum(grads.astype(F32), axis=0, keepdims=True)
    return dot(activations, grads, (1, 0)).astype(BF), bias


def both_cores(x):
    return lax.all_gather(x, "wid", axis_index_groups=CORE_GROUPS)


def body(activations, encoder, encoder_bias, decoder, decoder_bias, kept_mask, boundaries):
    tokens, width = activations.shape
    latents = encoder.shape[1]
    place = lax.axis_index("lat")
    core = lax.axis_index("wid") % N_CORE
    span = lax.axis_size("lat") // GROUPS
    group = place // span
    y, z = place // N_Z, place % N_Z
    late = z // NEAR >= N_FAR // 2
    my_slice = NEAR * y + (z - jnp.where(late, NEAR // 2, 0)) % NEAR
    half = (tokens // N_CORE, latents)
    half_low = [(half, BF)]
    many = [((N_X,) + half, BF)]
    rows_act = activations.T

    on_core = {'core': core}
    sides = both_cores(jnp.concatenate([encoder, lanes_of(1 - core, rows_act)], axis=1))
    (total,) = call(encode, many, on_core, sides, rows_act)
    decoder_rows, boundaries, total = lax.optimization_barrier((decoder.T, boundaries, total))

    has_cut = (place % span == 0) & (group > 0)
    cut = jnp.where(has_cut, boundaries[jnp.maximum(group - 1, 0)] - place * latents, 0)
    late = late.astype(jnp.int32)
    at_cut = {'cut': cut}

    pieces = swap(total, "wid", CHIP_GROUPS)
    decoders = both_cores(decoder_rows)
    (my_codes,) = call(kept_codes, half_low, on_core, pieces, kept_mask, encoder_bias[None])

    (got,) = call(decode, [((SLICES, ROWS, tokens), BF)], at_cut, my_codes, decoders)
    got = swap(got, "lat", NEAR_GROUPS)
    (got,) = call(near_sums, [((N_FAR, N_Y, ROWS, tokens), BF)], {}, got)
    later_act, later_bias, later_codes, got = lax.optimization_barrier((rows_act, decoder_bias, my_codes, got))
    got = swap(got, "lat", FAR_GROUPS)
    (base,) = call(own_base, [((PIECE, tokens), F32)], {'my_slice': my_slice}, later_act, later_bias[:, None])
    base, codes = both_cores(base), both_cores(later_codes)
    got, base, codes = lax.optimization_barrier((got, base, codes))
    (got,) = call(suffixes, [((SLICES, ROWS + TAG_ROWS, tokens), BF)], {'core': core, 'late': late}, got, base)
    got = swap(got, "lat", NEAR_GROUPS)

    (total,) = call(back, many, at_cut, got, decoders)
    got, total = lax.optimization_barrier((got, total))
    pieces = swap(total, "wid", CHIP_GROUPS)
    decoder_grad, tags = call(
        decoder_grads, [((width, latents), BF), ((SLICES, tokens), F32)], {'core': core, 'cut': cut}, both_cores(got), codes
    )
    decoder_bias_grad = tags[:, :PIECE].reshape(width)
    (my_grads,) = call(kept_grads, half_low, on_core, pieces, kept_mask)
    encoder_grad, encoder_bias_grad = call(
        encoder_grads, [((width, latents), BF), ((1, latents), F32)], {}, both_cores(my_grads), rows_act
    )
    return (encoder_grad, encoder_bias_grad.reshape(latents), decoder_grad.T, decoder_bias_grad)


def solution(mesh):
    placed = (
        P(None, "wid"),
        P("wid", "lat"),
        P("lat"),
        P("lat", "wid"),
        P("wid"),
        P(None, "lat"),
        P(),
    )
    return jax.shard_map(
        body,
        mesh=mesh,
        in_specs=placed,
        out_specs=(P("wid", "lat"), P("lat"), P("lat", "wid"), P("wid")),
        check_vma=False,
    )
```

```python
import collections

import jax
import jax.numpy as jnp
from jax import lax
from jax.experimental import pallas as pl
from jax.experimental.pallas import tpu as pltpu
from jax.sharding import PartitionSpec as P

GROUPS = 8
BF = jnp.bfloat16
F32 = jnp.float32

N_Y, N_FAR, NEAR = 4, 4, 4
N_Z = N_FAR * NEAR
SLICES = N_Y * NEAR
TURN = [0, 0, NEAR // 2, NEAR // 2]


def at(y, q, s):
    return N_Z * y + NEAR * q + (s + TURN[q]) % NEAR


NEAR_ORDER = [(3, 2), (0, 1), (0, 3), (3, 3), (2, 0), (0, 0), (1, 3), (2, 1), (1, 2), (1, 0), (3, 1), (1, 1), (2, 3), (0, 2), (3, 0), (2, 2)]
NEAR_GROUPS = [[at(y, q, s) for y, s in NEAR_ORDER] for q in range(N_FAR)]
FAR_GROUPS = [[at(y, q, s) for q in range(N_FAR)] for y, s in NEAR_ORDER]
PIECE = 28
ROWS = 2 * PIECE
TAG_ROWS = 8
N_CORE, N_X = 2, 4
CORE_GROUPS = [[N_CORE * x + c for c in range(N_CORE)] for x in range(N_X)]
CHIP_GROUPS = [[N_CORE * x + c for x in (0, 2, 1, 3)] for c in range(N_CORE)]


Scalars = collections.namedtuple('Scalars', ['core', 'late', 'cut', 'my_place'], defaults=(None,) * 4)


def swap(x, axis, groups=None):
    return lax.all_to_all(x, axis, 0, 0, axis_index_groups=groups, tiled=False)


def copies(x, count):
    return jnp.broadcast_to(x[None], (count,) + x.shape)


def dot(a, b, over):
    return lax.dot_general(a, b, (((over[0],), (over[1],)), ((), ())), preferred_element_type=F32)


def to_slices(first, second):
    rows = [[x[PIECE * i : PIECE * (i + 1)] for x in (first, second)] for i in range(SLICES)]
    return jnp.stack([jnp.concatenate(pair, axis=0) for pair in rows])


def from_slices(x, core):
    x = x.astype(F32)
    return jnp.concatenate([x[i, PIECE * core : PIECE * (core + 1)] for i in range(SLICES)], axis=0)


def call(stage, shapes, scalars, *arrays):
    names = list(scalars)
    n_out = len(shapes)

    def kernel(*refs):
        at = Scalars(**{name: ref[0] for name, ref in zip(names, refs)})
        outs = stage(at, *[ref[...] for ref in refs[len(names) : -n_out]])
        for ref, out in zip(refs[-n_out:], outs, strict=True):
            if isinstance(out, list):
                for i, one in enumerate(out):
                    ref[i] = one
            else:
                ref[...] = out

    vmem = pl.BlockSpec(memory_space=pltpu.VMEM)
    return pl.pallas_call(
        kernel,
        out_shape=[jax.ShapeDtypeStruct(shape, dtype) for shape, dtype in shapes],
        in_specs=[pl.BlockSpec(memory_space=pltpu.SMEM)] * len(names) + [vmem] * len(arrays),
        out_specs=[vmem] * n_out,
        compiler_params=pltpu.CompilerParams(vmem_limit_bytes=32 * 1024 * 1024),
        name=stage.__name__,
    )(*[scalars[name].reshape(1) for name in names], *arrays)


def half_of(core, x):
    half = x.shape[0] // N_CORE
    return jnp.where(core == 0, x[:half], x[half:])


def split_codes(codes, cut):
    codes = codes.astype(F32)
    below = lax.broadcasted_iota(jnp.int32, codes.shape, 1) < cut
    return jnp.concatenate([jnp.where(below, codes, 0.0), jnp.where(below, 0.0, codes)], axis=0).astype(BF)


def encode(_, activations, encoder):
    return (dot(activations, encoder, (0, 0)),)


def pair_sum(at, parts):
    return ([(half_of(at.core, parts[0]) + half_of(at.core, parts[1])).astype(BF)] * N_X,)


def kept_codes(at, pieces, mask, bias):
    total = jnp.sum(pieces.astype(F32), axis=0) + bias
    return ((half_of(at.core, mask).astype(F32) * total).astype(BF),)


def kept_grads(at, pieces, mask):
    return ((half_of(at.core, mask).astype(F32) * jnp.sum(pieces.astype(F32), axis=0)).astype(BF),)


def decode(at, codes, decoders):
    codes = split_codes(codes, at.cut)
    first, second = [dot(decoders[core], codes, (1, 1)) for core in range(N_CORE)]
    return (to_slices(first, second).astype(BF),)


def near_sums(_, got):
    got = got.astype(F32)
    sums = [sum(got[i] for i, (at_y, _) in enumerate(NEAR_ORDER) if at_y == y) for y in range(N_Y)]
    return ([jnp.stack(sums).astype(BF)] * N_FAR,)


def own_base(at, activations, bias):
    base = bias - activations.astype(F32)
    pieces = [
        jnp.where(at.my_place == NEAR * y + s, base[PIECE * i : PIECE * (i + 1)], 0.0) for i, (y, s) in enumerate(NEAR_ORDER)
    ]
    return (sum(pieces),)


def suffixes(at, got, bases):
    got = got.astype(F32)
    base = jnp.concatenate([bases[0], bases[1]], axis=0)
    half = base.shape[1] // 2

    def other_half(x):
        return pltpu.roll(x, half, 1)

    base = jnp.where(at.core == 0, other_half(base), base)
    run = base
    errors = []
    for y in range(N_Y):
        run = run + ((got[0, y] + got[1, y]) + other_half(got[2, y]))
        errors.append(run)
        part = got[2, y] + got[3, y]
        run = run + (part + other_half(got[0, y + 1]) if y + 1 < N_Y else part)
        errors.append(run)
    tail = jnp.zeros_like(base)
    suffix = []
    for error in reversed(errors):
        tail = tail + error
        suffix.append(tail / GROUPS)
    suffix = suffix[::-1]
    row = lax.broadcasted_iota(jnp.int32, base.shape, 0)
    lane = lax.broadcasted_iota(jnp.int32, base.shape, 1)
    token_sum = jnp.sum(jnp.where(lane < half, 0.0, suffix[0]), axis=1, keepdims=True)
    token_row = jnp.sum(jnp.where(row == lane, token_sum, 0.0), axis=0, keepdims=True)
    token_high = token_row.astype(BF).astype(F32)
    tag_row = lax.broadcasted_iota(jnp.int32, (TAG_ROWS, base.shape[1]), 0)
    tags = jnp.where(tag_row == 0, token_high, jnp.where(tag_row == 1, token_row - token_high, 0.0))
    out = []
    for y in range(N_Y):
        own = jnp.where(at.late == 1, suffix[2 * y + 1], suffix[2 * y])
        previous = jnp.where(at.late == 1, suffix[2 * y], suffix[max(2 * y - 1, 0)])
        pair = jnp.where(lane < half, other_half(previous), own)
        out.append(jnp.concatenate([pair, tags], axis=0).astype(BF))
    return ([out[y] for y, _ in NEAR_ORDER],)


def back(at, got, decoders):
    parts = [dot(from_slices(got, core).astype(BF), decoders[core], (0, 0)) for core in range(N_CORE)]
    total = parts[0] + parts[1]
    half = total.shape[0] // 2
    below = lax.broadcasted_iota(jnp.int32, (half, total.shape[1]), 1) < at.cut
    return ([jnp.where(below, total[:half], total[half:]).astype(BF)] * N_X,)


def decoder_grads(at, got, codes):
    total, tags = 0.0, 0.0
    for half in range(N_CORE):
        suffix = jnp.where(at.core == 0, from_slices(got[half], 0), from_slices(got[half], 1))
        total = total + dot(suffix.astype(BF), split_codes(codes[half], at.cut), (1, 0))
        tags = tags + jnp.sum(got[half, :, ROWS:].astype(F32), axis=1)
    tags = jnp.where(at.core == 0, tags, pltpu.roll(tags, tags.shape[1] - PIECE, 1))
    return total.astype(BF), tags


def encoder_grads(_, grads, activations):
    grads = jnp.concatenate([grads[0], grads[1]], axis=0)
    bias = jnp.sum(grads.astype(F32), axis=0, keepdims=True)
    return dot(activations, grads, (1, 0)).astype(BF), bias


def both_cores(x):
    return lax.all_gather(x, "wid", axis_index_groups=CORE_GROUPS)


def body(activations, encoder, encoder_bias, decoder, decoder_bias, kept_mask, boundaries):
    tokens, width = activations.shape
    latents = encoder.shape[1]
    place = lax.axis_index("lat")
    core = lax.axis_index("wid") % N_CORE
    span = lax.axis_size("lat") // GROUPS
    group = place // span
    y, z = place // N_Z, place % N_Z
    late = z // NEAR >= N_FAR // 2
    my_place = NEAR * y + (z - jnp.where(late, NEAR // 2, 0)) % NEAR
    half = (tokens // N_CORE, latents)
    half_low = [(half, BF)]
    many = [((N_X,) + half, BF)]
    rows_act = activations.T

    on_core = {'core': core}
    (enc_part,) = call(encode, [((tokens, latents), F32)], {}, rows_act, encoder)
    (total,) = call(pair_sum, many, on_core, both_cores(enc_part))
    decoder_rows, boundaries, total = lax.optimization_barrier((decoder.T, boundaries, total))

    has_cut = (place % span == 0) & (group > 0)
    cut = jnp.where(has_cut, boundaries[jnp.maximum(group - 1, 0)] - place * latents, 0)
    late = late.astype(jnp.int32)
    at_cut = {'cut': cut}

    pieces = swap(total, "wid", CHIP_GROUPS)
    decoders = both_cores(decoder_rows)
    (my_codes,) = call(kept_codes, half_low, on_core, pieces, kept_mask, encoder_bias[None])

    (got,) = call(decode, [((SLICES, ROWS, tokens), BF)], at_cut, my_codes, decoders)
    got = swap(got, "lat", NEAR_GROUPS)
    (got,) = call(near_sums, [((N_FAR, N_Y, ROWS, tokens), BF)], {}, got)
    later_act, later_bias, later_codes, got = lax.optimization_barrier((rows_act, decoder_bias, my_codes, got))
    got = swap(got, "lat", FAR_GROUPS)
    (base,) = call(own_base, [((PIECE, tokens), F32)], {'my_place': my_place}, later_act, later_bias[:, None])
    base, codes = both_cores(base), both_cores(later_codes)
    got, base, codes = lax.optimization_barrier((got, base, codes))
    (got,) = call(suffixes, [((SLICES, ROWS + TAG_ROWS, tokens), BF)], {'core': core, 'late': late}, got, base)
    got = swap(got, "lat", NEAR_GROUPS)

    (total,) = call(back, many, at_cut, got, decoders)
    got, total = lax.optimization_barrier((got, total))
    pieces = swap(total, "wid", CHIP_GROUPS)
    decoder_grad, tags = call(
        decoder_grads, [((width, latents), BF), ((SLICES, tokens), F32)], {'core': core, 'cut': cut}, both_cores(got), codes
    )
    decoder_bias_grad = tags[:, :PIECE].reshape(width)
    (my_grads,) = call(kept_grads, half_low, on_core, pieces, kept_mask)
    encoder_grad, encoder_bias_grad = call(
        encoder_grads, [((width, latents), BF), ((1, latents), F32)], {}, both_cores(my_grads), rows_act
    )
    return (encoder_grad, encoder_bias_grad.reshape(latents), decoder_grad.T, decoder_bias_grad)


def solution(mesh):
    placed = (
        P(None, "wid"),
        P("wid", "lat"),
        P("lat"),
        P("lat", "wid"),
        P("wid"),
        P(None, "lat"),
        P(),
    )
    return jax.shard_map(
        body,
        mesh=mesh,
        in_specs=placed,
        out_specs=(P("wid", "lat"), P("lat"), P("lat", "wid"), P("wid")),
        check_vma=False,
    )
```

```python
import collections

import jax
import jax.numpy as jnp
from jax import lax
from jax.experimental import pallas as pl
from jax.experimental.pallas import tpu as pltpu
from jax.sharding import PartitionSpec as P

GROUPS = 8
BF = jnp.bfloat16
F32 = jnp.float32

N_Y, N_FAR, NEAR = 4, 4, 4
N_Z = N_FAR * NEAR
SLICES = N_Y * NEAR
TURN = [0, 0, NEAR // 2, NEAR // 2]


def at(y, q, s):
    return N_Z * y + NEAR * q + (s + TURN[q]) % NEAR


NEAR_GROUPS = [[at(y, q, s) for y in range(N_Y) for s in range(NEAR)] for q in range(N_FAR)]
FAR_GROUPS = [[at(y, q, s) for q in range(N_FAR)] for y in range(N_Y) for s in range(NEAR)]
PIECE = 28
ROWS = 2 * PIECE
TAG_ROWS = 8
N_CORE, N_X = 2, 4
CORE_GROUPS = [[N_CORE * x + c for c in range(N_CORE)] for x in range(N_X)]
CHIP_GROUPS = [[N_CORE * x + c for x in range(N_X)] for c in range(N_CORE)]


Scalars = collections.namedtuple('Scalars', ['core', 'late', 'cut', 'my_slice'], defaults=(None,) * 4)


def swap(x, axis, groups=None):
    return lax.all_to_all(x, axis, 0, 0, axis_index_groups=groups, tiled=False)


def copies(x, count):
    return jnp.broadcast_to(x[None], (count,) + x.shape)


def dot(a, b, over):
    return lax.dot_general(a, b, (((over[0],), (over[1],)), ((), ())), preferred_element_type=F32)


def to_slices(first, second):
    rows = [[x[PIECE * i : PIECE * (i + 1)] for x in (first, second)] for i in range(SLICES)]
    return jnp.stack([jnp.concatenate(pair, axis=0) for pair in rows])


def from_slices(x, core):
    x = x.astype(F32)
    return jnp.concatenate([x[i, PIECE * core : PIECE * (core + 1)] for i in range(SLICES)], axis=0)


def call(stage, shapes, scalars, *arrays):
    names = list(scalars)
    n_out = len(shapes)

    def kernel(*refs):
        at = Scalars(**{name: ref[0] for name, ref in zip(names, refs)})
        outs = stage(at, *[ref[...] for ref in refs[len(names) : -n_out]])
        for ref, out in zip(refs[-n_out:], outs, strict=True):
            if isinstance(out, list):
                for i, one in enumerate(out):
                    ref[i] = one
            else:
                ref[...] = out

    vmem = pl.BlockSpec(memory_space=pltpu.VMEM)
    return pl.pallas_call(
        kernel,
        out_shape=[jax.ShapeDtypeStruct(shape, dtype) for shape, dtype in shapes],
        in_specs=[pl.BlockSpec(memory_space=pltpu.SMEM)] * len(names) + [vmem] * len(arrays),
        out_specs=[vmem] * n_out,
        compiler_params=pltpu.CompilerParams(vmem_limit_bytes=32 * 1024 * 1024),
        name=stage.__name__,
    )(*[scalars[name].reshape(1) for name in names], *arrays)


def half_of(core, x):
    half = x.shape[0] // N_CORE
    return jnp.where(core == 0, x[:half], x[half:])


def split_codes(codes, cut):
    codes = codes.astype(F32)
    below = lax.broadcasted_iota(jnp.int32, codes.shape, 1) < cut
    return jnp.concatenate([jnp.where(below, codes, 0.0), jnp.where(below, 0.0, codes)], axis=0).astype(BF)


def pair_sum(at, parts):
    return ([(half_of(at.core, parts[0]) + half_of(at.core, parts[1])).astype(BF)] * N_X,)


def kept_codes(at, pieces, mask, bias):
    total = jnp.sum(pieces.astype(F32), axis=0) + bias
    return ((half_of(at.core, mask).astype(F32) * total).astype(BF),)


def kept_grads(at, pieces, mask):
    return ((half_of(at.core, mask).astype(F32) * jnp.sum(pieces.astype(F32), axis=0)).astype(BF),)


def decode(at, codes, decoders):
    codes = split_codes(codes, at.cut)
    first, second = [dot(decoders[core], codes, (1, 1)) for core in range(N_CORE)]
    return (to_slices(first, second).astype(BF),)


def near_sums(_, got):
    tokens = got.shape[-1]
    got = got.astype(F32).reshape(N_Y, NEAR, ROWS, tokens)
    return ([jnp.sum(got, axis=1).astype(BF)] * N_FAR,)


def own_base(at, activations, bias):
    base = bias - activations.astype(F32)
    pieces = [jnp.where(at.my_slice == i, base[PIECE * i : PIECE * (i + 1)], 0.0) for i in range(SLICES)]
    return (sum(pieces),)


def suffixes(at, got, bases):
    got = got.astype(F32)
    base = jnp.concatenate([bases[0], bases[1]], axis=0)
    half = base.shape[1] // 2

    def other_half(x):
        return pltpu.roll(x, half, 1)

    base = jnp.where(at.core == 0, other_half(base), base)
    run = base
    errors = []
    for y in range(N_Y):
        run = run + ((got[0, y] + got[1, y]) + other_half(got[2, y]))
        errors.append(run)
        part = got[2, y] + got[3, y]
        run = run + (part + other_half(got[0, y + 1]) if y + 1 < N_Y else part)
        errors.append(run)
    tail = jnp.zeros_like(base)
    suffix = []
    for error in reversed(errors):
        tail = tail + error
        suffix.append(tail / GROUPS)
    suffix = suffix[::-1]
    row = lax.broadcasted_iota(jnp.int32, base.shape, 0)
    lane = lax.broadcasted_iota(jnp.int32, base.shape, 1)
    token_sum = jnp.sum(jnp.where(lane < half, 0.0, suffix[0]), axis=1, keepdims=True)
    token_row = jnp.sum(jnp.where(row == lane, token_sum, 0.0), axis=0, keepdims=True)
    token_high = token_row.astype(BF).astype(F32)
    tag_row = lax.broadcasted_iota(jnp.int32, (TAG_ROWS, base.shape[1]), 0)
    tags = jnp.where(tag_row == 0, token_high, jnp.where(tag_row == 1, token_row - token_high, 0.0))
    out = []
    for y in range(N_Y):
        own = jnp.where(at.late == 1, suffix[2 * y + 1], suffix[2 * y])
        previous = jnp.where(at.late == 1, suffix[2 * y], suffix[max(2 * y - 1, 0)])
        pair = jnp.where(lane < half, other_half(previous), own)
        out += [jnp.concatenate([pair, tags], axis=0).astype(BF)] * NEAR
    return (out,)


def back(at, got, decoders):
    parts = [dot(from_slices(got, core).astype(BF), decoders[core], (0, 0)) for core in range(N_CORE)]
    total = parts[0] + parts[1]
    half = total.shape[0] // 2
    below = lax.broadcasted_iota(jnp.int32, (half, total.shape[1]), 1) < at.cut
    return ([jnp.where(below, total[:half], total[half:]).astype(BF)] * N_X,)


def decoder_grads(at, got, codes):
    total, tags = 0.0, 0.0
    for half in range(N_CORE):
        suffix = jnp.where(at.core == 0, from_slices(got[half], 0), from_slices(got[half], 1))
        total = total + dot(suffix.astype(BF), split_codes(codes[half], at.cut), (1, 0))
        tags = tags + jnp.sum(got[half, :, ROWS:].astype(F32), axis=1)
    tags = jnp.where(at.core == 0, tags, pltpu.roll(tags, tags.shape[1] - PIECE, 1))
    return total.astype(BF), tags


def encoder_grads(_, grads, activations):
    grads = jnp.concatenate([grads[0], grads[1]], axis=0)
    bias = jnp.sum(grads.astype(F32), axis=0, keepdims=True)
    return dot(activations, grads, (1, 0)).astype(BF), bias


def both_cores(x):
    return lax.all_gather(x, "wid", axis_index_groups=CORE_GROUPS)


def body(activations, encoder, encoder_bias, decoder, decoder_bias, kept_mask, boundaries):
    tokens, width = activations.shape
    latents = encoder.shape[1]
    place = lax.axis_index("lat")
    core = lax.axis_index("wid") % N_CORE
    span = lax.axis_size("lat") // GROUPS
    group = place // span
    y, z = place // N_Z, place % N_Z
    late = z // NEAR >= N_FAR // 2
    my_slice = NEAR * y + (z - jnp.where(late, NEAR // 2, 0)) % NEAR
    half = (tokens // N_CORE, latents)
    half_low = [(half, BF)]
    many = [((N_X,) + half, BF)]
    rows_act = activations.T

    on_core = {'core': core}
    enc_part = dot(activations, encoder, (1, 0))
    (total,) = call(pair_sum, many, on_core, both_cores(enc_part))
    decoder_rows, boundaries, total = lax.optimization_barrier((decoder.T, boundaries, total))

    has_cut = (place % span == 0) & (group > 0)
    cut = jnp.where(has_cut, boundaries[jnp.maximum(group - 1, 0)] - place * latents, 0)
    late = late.astype(jnp.int32)
    at_cut = {'cut': cut}

    pieces = swap(total, "wid", CHIP_GROUPS)
    decoders = both_cores(decoder_rows)
    (my_codes,) = call(kept_codes, half_low, on_core, pieces, kept_mask, encoder_bias[None])

    (got,) = call(decode, [((SLICES, ROWS, tokens), BF)], at_cut, my_codes, decoders)
    got = swap(got, "lat", NEAR_GROUPS)
    (got,) = call(near_sums, [((N_FAR, N_Y, ROWS, tokens), BF)], {}, got)
    later_act, later_bias, later_codes, got = lax.optimization_barrier((rows_act, decoder_bias, my_codes, got))
    got = swap(got, "lat", FAR_GROUPS)
    (base,) = call(own_base, [((PIECE, tokens), F32)], {'my_slice': my_slice}, later_act, later_bias[:, None])
    base, codes = both_cores(base), both_cores(later_codes)
    got, base, codes = lax.optimization_barrier((got, base, codes))
    (got,) = call(suffixes, [((SLICES, ROWS + TAG_ROWS, tokens), BF)], {'core': core, 'late': late}, got, base)
    got = swap(got, "lat", NEAR_GROUPS)

    (total,) = call(back, many, at_cut, got, decoders)
    got, total = lax.optimization_barrier((got, total))
    pieces = swap(total, "wid", CHIP_GROUPS)
    decoder_grad, tags = call(
        decoder_grads, [((width, latents), BF), ((SLICES, tokens), F32)], {'core': core, 'cut': cut}, both_cores(got), codes
    )
    decoder_bias_grad = tags[:, :PIECE].reshape(width)
    (my_grads,) = call(kept_grads, half_low, on_core, pieces, kept_mask)
    encoder_grad, encoder_bias_grad = call(
        encoder_grads, [((width, latents), BF), ((1, latents), F32)], {}, both_cores(my_grads), rows_act
    )
    return (encoder_grad, encoder_bias_grad.reshape(latents), decoder_grad.T, decoder_bias_grad)


def solution(mesh):
    placed = (
        P(None, "wid"),
        P("wid", "lat"),
        P("lat"),
        P("lat", "wid"),
        P("wid"),
        P(None, "lat"),
        P(),
    )
    return jax.shard_map(
        body,
        mesh=mesh,
        in_specs=placed,
        out_specs=(P("wid", "lat"), P("lat"), P("lat", "wid"), P("wid")),
        check_vma=False,
    )
```

```python
import collections

import jax
import jax.numpy as jnp
from jax import lax
from jax.experimental import pallas as pl
from jax.experimental.pallas import tpu as pltpu
from jax.sharding import PartitionSpec as P

GROUPS = 8
BF = jnp.bfloat16
F32 = jnp.float32

N_Y, N_FAR, NEAR = 4, 4, 4
N_Z = N_FAR * NEAR
SLICES = N_Y * NEAR
TURN = [0, 0, NEAR // 2, NEAR // 2]


def at(y, q, s):
    return N_Z * y + NEAR * q + (s + TURN[q]) % NEAR


NEAR_GROUPS = [[at(y, q, s) for y in range(N_Y) for s in range(NEAR)] for q in range(N_FAR)]
FAR_GROUPS = [[at(y, q, s) for q in range(N_FAR)] for y in range(N_Y) for s in range(NEAR)]
PIECE = 28
ROWS = 2 * PIECE
TAG_ROWS = 8
N_CORE, N_X = 2, 4
CORE_GROUPS = [[N_CORE * x + c for c in range(N_CORE)] for x in range(N_X)]
CHIP_GROUPS = [[N_CORE * x + c for x in range(N_X)] for c in range(N_CORE)]


Scalars = collections.namedtuple('Scalars', ['core', 'late', 'cut', 'my_slice'], defaults=(None,) * 4)


def swap(x, axis, groups=None):
    return lax.all_to_all(x, axis, 0, 0, axis_index_groups=groups, tiled=False)


def copies(x, count):
    return jnp.broadcast_to(x[None], (count,) + x.shape)


def dot(a, b, over):
    return lax.dot_general(a, b, (((over[0],), (over[1],)), ((), ())), preferred_element_type=F32)


def to_slices(first, second):
    rows = [[x[PIECE * i : PIECE * (i + 1)] for x in (first, second)] for i in range(SLICES)]
    return jnp.stack([jnp.concatenate(pair, axis=0) for pair in rows])


def from_slices(x, core):
    x = x.astype(F32)
    return jnp.concatenate([x[i, PIECE * core : PIECE * (core + 1)] for i in range(SLICES)], axis=0)


def call(stage, shapes, scalars, *arrays):
    names = list(scalars)
    n_out = len(shapes)

    def kernel(*refs):
        at = Scalars(**{name: ref[0] for name, ref in zip(names, refs)})
        outs = stage(at, *[ref[...] for ref in refs[len(names) : -n_out]])
        for ref, out in zip(refs[-n_out:], outs, strict=True):
            if isinstance(out, list):
                for i, one in enumerate(out):
                    ref[i] = one
            else:
                ref[...] = out

    vmem = pl.BlockSpec(memory_space=pltpu.VMEM)
    return pl.pallas_call(
        kernel,
        out_shape=[jax.ShapeDtypeStruct(shape, dtype) for shape, dtype in shapes],
        in_specs=[pl.BlockSpec(memory_space=pltpu.SMEM)] * len(names) + [vmem] * len(arrays),
        out_specs=[vmem] * n_out,
        compiler_params=pltpu.CompilerParams(vmem_limit_bytes=32 * 1024 * 1024),
        name=stage.__name__,
    )(*[scalars[name].reshape(1) for name in names], *arrays)


def half_of(core, x):
    half = x.shape[0] // N_CORE
    return jnp.where(core == 0, x[:half], x[half:])


def split_codes(codes, cut):
    codes = codes.astype(F32)
    below = lax.broadcasted_iota(jnp.int32, codes.shape, 1) < cut
    return jnp.concatenate([jnp.where(below, codes, 0.0), jnp.where(below, 0.0, codes)], axis=0).astype(BF)


def pair_sum(at, parts):
    return ([(half_of(at.core, parts[0]) + half_of(at.core, parts[1])).astype(BF)] * N_X,)


def kept_codes(at, pieces, mask, bias):
    total = jnp.sum(pieces.astype(F32), axis=0) + bias
    return ((half_of(at.core, mask).astype(F32) * total).astype(BF),)


def kept_grads(at, pieces, mask):
    return ((half_of(at.core, mask).astype(F32) * jnp.sum(pieces.astype(F32), axis=0)).astype(BF),)


def decode(at, pieces, mask, bias, decoders):
    (my_codes,) = kept_codes(at, pieces, mask, bias)
    codes = split_codes(my_codes, at.cut)
    first, second = [dot(decoders[core], codes, (1, 1)) for core in range(N_CORE)]
    return to_slices(first, second).astype(BF), my_codes


def near_sums(_, got):
    tokens = got.shape[-1]
    got = got.astype(F32).reshape(N_Y, NEAR, ROWS, tokens)
    return ([jnp.sum(got, axis=1).astype(BF)] * N_FAR,)


def own_base(at, activations, bias):
    base = bias - activations.astype(F32)
    pieces = [jnp.where(at.my_slice == i, base[PIECE * i : PIECE * (i + 1)], 0.0) for i in range(SLICES)]
    return (sum(pieces),)


def suffixes(at, got, bases):
    got = got.astype(F32)
    base = jnp.concatenate([bases[0], bases[1]], axis=0)
    half = base.shape[1] // 2

    def other_half(x):
        return pltpu.roll(x, half, 1)

    base = jnp.where(at.core == 0, other_half(base), base)
    run = base
    errors = []
    for y in range(N_Y):
        run = run + ((got[0, y] + got[1, y]) + other_half(got[2, y]))
        errors.append(run)
        part = got[2, y] + got[3, y]
        run = run + (part + other_half(got[0, y + 1]) if y + 1 < N_Y else part)
        errors.append(run)
    tail = jnp.zeros_like(base)
    suffix = []
    for error in reversed(errors):
        tail = tail + error
        suffix.append(tail / GROUPS)
    suffix = suffix[::-1]
    row = lax.broadcasted_iota(jnp.int32, base.shape, 0)
    lane = lax.broadcasted_iota(jnp.int32, base.shape, 1)
    token_sum = jnp.sum(jnp.where(lane < half, 0.0, suffix[0]), axis=1, keepdims=True)
    token_row = jnp.sum(jnp.where(row == lane, token_sum, 0.0), axis=0, keepdims=True)
    token_high = token_row.astype(BF).astype(F32)
    tag_row = lax.broadcasted_iota(jnp.int32, (TAG_ROWS, base.shape[1]), 0)
    tags = jnp.where(tag_row == 0, token_high, jnp.where(tag_row == 1, token_row - token_high, 0.0))
    out = []
    for y in range(N_Y):
        own = jnp.where(at.late == 1, suffix[2 * y + 1], suffix[2 * y])
        previous = jnp.where(at.late == 1, suffix[2 * y], suffix[max(2 * y - 1, 0)])
        pair = jnp.where(lane < half, other_half(previous), own)
        out += [jnp.concatenate([pair, tags], axis=0).astype(BF)] * NEAR
    return (out,)


def back(at, got, decoders):
    parts = [dot(from_slices(got, core).astype(BF), decoders[core], (0, 0)) for core in range(N_CORE)]
    total = parts[0] + parts[1]
    half = total.shape[0] // 2
    below = lax.broadcasted_iota(jnp.int32, (half, total.shape[1]), 1) < at.cut
    return ([jnp.where(below, total[:half], total[half:]).astype(BF)] * N_X,)


def decoder_grads(at, got, codes):
    total, tags = 0.0, 0.0
    for half in range(N_CORE):
        suffix = jnp.where(at.core == 0, from_slices(got[half], 0), from_slices(got[half], 1))
        total = total + dot(suffix.astype(BF), split_codes(codes[half], at.cut), (1, 0))
        tags = tags + jnp.sum(got[half, :, ROWS:].astype(F32), axis=1)
    tags = jnp.where(at.core == 0, tags, pltpu.roll(tags, tags.shape[1] - PIECE, 1))
    return total.astype(BF), tags


def encoder_grads(_, grads, activations):
    grads = jnp.concatenate([grads[0], grads[1]], axis=0)
    bias = jnp.sum(grads.astype(F32), axis=0, keepdims=True)
    return dot(activations, grads, (1, 0)).astype(BF), bias


def both_cores(x):
    return lax.all_gather(x, "wid", axis_index_groups=CORE_GROUPS)


def body(activations, encoder, encoder_bias, decoder, decoder_bias, kept_mask, boundaries):
    tokens, width = activations.shape
    latents = encoder.shape[1]
    place = lax.axis_index("lat")
    core = lax.axis_index("wid") % N_CORE
    span = lax.axis_size("lat") // GROUPS
    group = place // span
    y, z = place // N_Z, place % N_Z
    late = z // NEAR >= N_FAR // 2
    my_slice = NEAR * y + (z - jnp.where(late, NEAR // 2, 0)) % NEAR
    half = (tokens // N_CORE, latents)
    half_low = [(half, BF)]
    many = [((N_X,) + half, BF)]
    rows_act = activations.T

    on_core = {'core': core}
    enc_part = dot(activations, encoder, (1, 0))
    (total,) = call(pair_sum, many, on_core, both_cores(enc_part))
    decoder_rows, boundaries, total = lax.optimization_barrier((decoder.T, boundaries, total))

    has_cut = (place % span == 0) & (group > 0)
    cut = jnp.where(has_cut, boundaries[jnp.maximum(group - 1, 0)] - place * latents, 0)
    late = late.astype(jnp.int32)
    at_cut = {'cut': cut}

    pieces = swap(total, "wid", CHIP_GROUPS)
    decoders = both_cores(decoder_rows)

    got, my_codes = call(
        decode, [((SLICES, ROWS, tokens), BF)] + half_low, on_core | at_cut, pieces, kept_mask, encoder_bias[None], decoders
    )
    got = swap(got, "lat", NEAR_GROUPS)
    (got,) = call(near_sums, [((N_FAR, N_Y, ROWS, tokens), BF)], {}, got)
    later_act, later_bias, later_codes, got = lax.optimization_barrier((rows_act, decoder_bias, my_codes, got))
    got = swap(got, "lat", FAR_GROUPS)
    (base,) = call(own_base, [((PIECE, tokens), F32)], {'my_slice': my_slice}, later_act, later_bias[:, None])
    base, codes = both_cores(base), both_cores(later_codes)
    got, base, codes = lax.optimization_barrier((got, base, codes))
    (got,) = call(suffixes, [((SLICES, ROWS + TAG_ROWS, tokens), BF)], {'core': core, 'late': late}, got, base)
    got = swap(got, "lat", NEAR_GROUPS)

    (total,) = call(back, many, at_cut, got, decoders)
    got, total = lax.optimization_barrier((got, total))
    pieces = swap(total, "wid", CHIP_GROUPS)
    decoder_grad, tags = call(
        decoder_grads, [((width, latents), BF), ((SLICES, tokens), F32)], {'core': core, 'cut': cut}, both_cores(got), codes
    )
    decoder_bias_grad = tags[:, :PIECE].reshape(width)
    (my_grads,) = call(kept_grads, half_low, on_core, pieces, kept_mask)
    encoder_grad, encoder_bias_grad = call(
        encoder_grads, [((width, latents), BF), ((1, latents), F32)], {}, both_cores(my_grads), rows_act
    )
    return (encoder_grad, encoder_bias_grad.reshape(latents), decoder_grad.T, decoder_bias_grad)


def solution(mesh):
    placed = (
        P(None, "wid"),
        P("wid", "lat"),
        P("lat"),
        P("lat", "wid"),
        P("wid"),
        P(None, "lat"),
        P(),
    )
    return jax.shard_map(
        body,
        mesh=mesh,
        in_specs=placed,
        out_specs=(P("wid", "lat"), P("lat"), P("lat", "wid"), P("wid")),
        check_vma=False,
    )
```
